256 devices in a mesh: section: 32 (over x, z_lo, core), tensor: 8 (over z_hi, y).
Axes of the slice: x: 4, y: 4, z: 8 (z_hi: 2, z_lo: 4; z = z_hi * 4 + z_lo), core: 2. Of those that a mesh axis runs over, the one named last changes fastest.
Arguments:
- activations: bfloat16 [32, 256, 4096], P('section', 'tensor'), may hold values from -6 to 6
- upstream_grad: bfloat16 [32, 256, 4096], P('section', 'tensor'), may hold values from -6 to 6
- stash_blocks: bfloat16 [32, 256, 4096], P('section', 'tensor'), may hold values from -6 to 6
- guest_blocks: bfloat16 [32, 256, 4096], P('section', 'tensor'), may hold values from -6 to 6
- norm_gain: float32 [32, 4096], P('section'), may hold values from 0.1 to 1.9
- query_weight: bfloat16 [32, 4096, 4096], P('section', None, 'tensor'), may hold values from -2 to 2
- keyval_weight: bfloat16 [32, 4096, 2, 1024], P('section', None, None, 'tensor'), may hold values from -1 to 1
- output_weight: bfloat16 [32, 4096, 4096], P('section', 'tensor'), may hold values from -0.09375 to 0.09375
- evict_marks: int32 [32, 16], replicated, may hold values from 0 to 1, as said below
Outputs:
- next_input: bfloat16 [32, 256, 4096], P('section', 'tensor')
- prev_grad: bfloat16 [32, 256, 4096], P('section', 'tensor')
- kept_stash: bfloat16 [32, 256, 4096], P('section', 'tensor')
- held_blocks: bfloat16 [32, 256, 4096], P('section', 'tensor')
The draws below stay inside these ranges and needn't reach their ends.
Inputs may be any that keep to these rules, and one draw needn't show every extreme that they name: `evict_marks`: row s marks with 1 the blocks that section s evicts to section 31 - s; a row has at most 8 ones, row 0 exactly 8, rows of the first half of the sections at least 4.
All inputs are finite; a program needn't handle non-finite values.
Results may differ from the reference program's by a relative error of at most 0.012.
Values may be sent and summed in bfloat16 or wider, within the bound.
A program may use at most 64 MiB of HBM per device.

```python
import math
import jax
import jax.numpy as jnp
from jax import lax

WIDTH = 4096
HEADS = 32
KV_HEADS = 8
HEAD_DIM = 128
TOK = 256
BLOCKS = 16
MOST_EVICT = 8
SECTIONS = 32
N_TENSOR = 8


def weight_pair(key):
    keyval_key = jax.random.fold_in(key, 11)
    query_key = jax.random.fold_in(key, 12)
    keyval = jax.random.normal(keyval_key, (SECTIONS, WIDTH, 2, KV_HEADS * HEAD_DIM), jnp.float32) / math.sqrt(WIDTH)
    noise_part = jax.random.normal(query_key, (SECTIONS, WIDTH, HEADS * HEAD_DIM), jnp.float32) / math.sqrt(WIDTH)
    return (keyval, noise_part)


def draw_keyval_weight(key, part):
    keyval, noise_part = weight_pair(key)
    return keyval.astype(jnp.bfloat16)


def draw_query_weight(key, part):
    keyval, noise_part = weight_pair(key)
    return noise_part.astype(jnp.bfloat16)


def draw_evict_marks(key, part):
    count_key = jax.random.fold_in(key, 21)
    order_key = jax.random.fold_in(key, 22)
    base_count = jax.random.randint(count_key, (SECTIONS,), 0, MOST_EVICT // 2 + 1)
    early_extra = jnp.where(jnp.arange(SECTIONS) < SECTIONS // 2, MOST_EVICT - MOST_EVICT // 2, 0)
    counts = jnp.minimum(base_count + early_extra, MOST_EVICT)
    counts = counts.at[0].set(MOST_EVICT)
    block_order = jax.vmap(lambda section_key: jax.random.permutation(section_key, BLOCKS))(jax.random.split(order_key, SECTIONS))
    return (block_order < counts[:, None]).astype(jnp.int32)


def steps_of(own_key, dims, cuts, least, top_value):
    loudness, own = 1.0, jax.random.fold_in(own_key, 6)
    for dim, shards_of in cuts:
        draws = jnp.exp(jax.random.uniform(jax.random.fold_in(own, dim), (shards_of,), jnp.float32, least / len(cuts), top_value / len(cuts)))
        loudness = loudness * jnp.repeat(draws, dims[dim] // shards_of).reshape([-1 if axis == dim else 1 for axis in range(len(dims))])
    return loudness


def gaussian(own_key, dims, scale, bound, pieces=(), held_as=jnp.bfloat16):
    level = steps_of(own_key, dims, pieces, -0.22, 0.18) if pieces else 1.0
    result = jax.random.normal(own_key, dims, jnp.float32) * scale * level
    return jnp.minimum(jnp.maximum(result, -bound), bound).astype(held_as)


def setup_inputs(seed: int = 0) -> dict:
    splits = jax.random.split(jax.random.key(seed), 10)
    return {
        "activations": gaussian(splits[0], (SECTIONS, TOK, WIDTH), 1.0, 6.0, ((0, 32), (1, 8))),
        "upstream_grad": gaussian(splits[1], (SECTIONS, TOK, WIDTH), 1.0, 6.0, ((0, 32), (1, 8))),
        "stash_blocks": gaussian(splits[2], (SECTIONS, TOK, WIDTH), 1.0, 6.0, ((0, 32), (1, 8))),
        "guest_blocks": gaussian(splits[3], (SECTIONS, TOK, WIDTH), 1.0, 6.0, ((0, 32), (1, 8))),
        "norm_gain": jnp.clip(1.0 + 0.18 * jax.random.normal(splits[4], (SECTIONS, WIDTH), jnp.float32), 0.1, 1.9),
        "query_weight": draw_query_weight(jax.random.fold_in(splits[9], 71), 0),
        "keyval_weight": draw_keyval_weight(jax.random.fold_in(splits[9], 71), 0),
        "output_weight": gaussian(splits[7], (SECTIONS, HEADS * HEAD_DIM, WIDTH), (HEADS * HEAD_DIM) ** -0.5, 0.09375, ((0, 32), (1, 8))),
        "evict_marks": draw_evict_marks(jax.random.fold_in(splits[9], 71), 0),
    }


EPSILON = 1e-05
NEG_LARGE = -1e+30

def root_norm(features, gain_row):
    values = features.astype(jnp.float32)
    factor = lax.rsqrt(lax.optimization_barrier(jnp.mean(values * values, axis=-1, keepdims=True)) + EPSILON)
    return values * factor * gain_row

def settle(values):
    return lax.optimization_barrier(values.astype(jnp.bfloat16))

def causal_probs(scores):
    length = scores.shape[-1]
    allowed = jnp.arange(length)[:, None] >= jnp.arange(length)[None, :]
    masked = jnp.where(allowed, scores, NEG_LARGE)
    row_max = lax.optimization_barrier(jnp.max(masked, axis=-1, keepdims=True))
    raised = jnp.exp(masked - row_max)
    return raised / lax.optimization_barrier(jnp.sum(raised, axis=-1, keepdims=True))

def one_section(current, back_rows, upstream, gain_row, query_weight, keyval_weight, output_weight):
    length = current.shape[0]
    group_size = HEADS // KV_HEADS
    head_scale = HEAD_DIM ** (-0.5)
    query_cols = HEADS * HEAD_DIM // N_TENSOR
    keyval_cols = KV_HEADS * HEAD_DIM // N_TENSOR
    keyval_flat = keyval_weight.reshape(WIDTH, 2 * KV_HEADS * HEAD_DIM)

    def project(normed):
        queries = settle(jnp.dot(normed, query_weight, preferred_element_type=jnp.float32))
        keyvals = settle(jnp.dot(normed, keyval_flat, preferred_element_type=jnp.float32))
        queries = queries.astype(jnp.float32).reshape(length, KV_HEADS, group_size, HEAD_DIM)
        keyvals = keyvals.astype(jnp.float32).reshape(length, 2, KV_HEADS, HEAD_DIM)
        return (queries, keyvals[:, 0], keyvals[:, 1])

    def scores_of(queries, key_rows):
        return causal_probs(jnp.einsum('tkgh,ukh->kgtu', queries, key_rows) * head_scale)
    normed_now = root_norm(current, gain_row).astype(jnp.bfloat16)
    normed_back = root_norm(back_rows, gain_row).astype(jnp.bfloat16)
    query_now, key_now, value_now = project(normed_now)
    probs_now = scores_of(query_now, key_now)
    weights_now = settle(probs_now).astype(jnp.float32)
    context_now = settle(jnp.einsum('kgtu,ukh->tkgh', weights_now, value_now)).astype(jnp.float32)
    context_groups = context_now.reshape(length, N_TENSOR, query_cols)
    out_groups = output_weight.astype(jnp.float32).reshape(N_TENSOR, query_cols, WIDTH)
    forward_parts = settle(jnp.einsum('tnc,ncd->ntd', context_groups, out_groups)).astype(jnp.float32)
    forward_sum = lax.optimization_barrier(jnp.sum(forward_parts, axis=0))
    updated = (current.astype(jnp.float32) + forward_sum).astype(jnp.bfloat16)
    query_back, key_back, value_back = project(normed_back)
    probs_back = scores_of(query_back, key_back)
    weights_back = settle(probs_back).astype(jnp.float32)
    grad_context = settle(jnp.einsum('td,cd->tc', upstream.astype(jnp.float32), output_weight.astype(jnp.float32)))
    grad_context = grad_context.astype(jnp.float32).reshape(length, KV_HEADS, group_size, HEAD_DIM)
    grad_value = settle(jnp.einsum('kgtu,tkgh->ukh', weights_back, grad_context)).astype(jnp.float32)
    grad_prob = jnp.einsum('tkgh,ukh->kgtu', grad_context, value_back)
    grad_score = probs_back * (grad_prob - lax.optimization_barrier(jnp.sum(probs_back * grad_prob, axis=-1, keepdims=True))) * head_scale
    grad_score = settle(grad_score).astype(jnp.float32)
    grad_query = settle(jnp.einsum('kgtu,ukh->tkgh', grad_score, key_back)).astype(jnp.float32)
    grad_key = settle(jnp.einsum('kgtu,tkgh->ukh', grad_score, query_back)).astype(jnp.float32)
    grad_keyval = jnp.stack([grad_key, grad_value], axis=1).reshape(length, 2, N_TENSOR, keyval_cols)
    query_groups = query_weight.astype(jnp.float32).reshape(WIDTH, N_TENSOR, query_cols)
    keyval_groups = keyval_weight.astype(jnp.float32).reshape(WIDTH, 2, N_TENSOR, keyval_cols)
    backward_parts = jnp.einsum('tnc,dnc->ntd', grad_query.reshape(length, N_TENSOR, query_cols), query_groups)
    backward_parts = backward_parts + jnp.einsum('tjnc,djnc->ntd', grad_keyval, keyval_groups)
    backward_sum = lax.optimization_barrier(jnp.sum(settle(backward_parts).astype(jnp.float32), axis=0))
    normed_out, pull_back = jax.vjp(lambda inputs: root_norm(inputs, gain_row), back_rows.astype(jnp.float32))
    norm_grad = pull_back(backward_sum)[0]
    passed = (upstream.astype(jnp.float32) + norm_grad).astype(jnp.bfloat16)
    return (updated, passed)

def reference(activations, upstream_grad, stash_blocks, guest_blocks, norm_gain, query_weight, keyval_weight, output_weight, evict_marks):
    row_count = TOK // N_TENSOR
    block_rows = row_count // BLOCKS
    token_marks = jnp.broadcast_to(evict_marks[:, None, :, None], (SECTIONS, N_TENSOR, BLOCKS, block_rows)).reshape(SECTIONS, TOK)
    moved = (token_marks == 1)[:, :, None]
    back_rows = jnp.where(moved, guest_blocks[::-1], stash_blocks)

    def run_section(inputs):
        return one_section(*inputs)
    updated, passed = lax.map(run_section, (activations, back_rows, upstream_grad, norm_gain, query_weight, keyval_weight, output_weight))
    zero_section = jnp.zeros_like(activations[:1])
    next_input = jnp.concatenate([zero_section, updated[:-1]], axis=0)
    prev_grad = jnp.concatenate([passed[1:], zero_section], axis=0)
    zero_all = jnp.zeros_like(activations)
    kept_stash = jnp.where(moved, zero_all, activations)
    held_blocks = jnp.where(moved, activations, zero_all)[::-1]
    return (next_input, prev_grad, kept_stash, held_blocks)
```

```python
import jax
import jax.numpy as jnp
from jax import lax
from jax.experimental import pallas as pl
from jax.experimental.pallas import tpu as pltpu
from jax.sharding import PartitionSpec as P

HEADS = 32
KV_HEADS = 8
HEAD_DIM = 128
GROUP = HEADS // KV_HEADS
EPSILON = 1e-05
NEG_LARGE = -1e30
MESH = pl.DeviceIdType.MESH
F32 = jnp.float32
BF16 = jnp.bfloat16

ROWS = 32
WIDTH = 4096
HALF = WIDTH // 2
BLOCKS = 16
PACKED = 16
CHUNKS = 2
CHUNK = ROWS // CHUNKS
QCOLS = 512
CCOLS = 768
LENGTH = 256
NOW, UP, BACK = 0, 1, 2


def copy_numbers():
    names = []
    for tensor in range(3):
        names.append(("z", tensor))
        for tag in range(2):
            for way in range(2):
                names.append(("y", tensor, tag, way))
                names.append(("half", tensor, tag, way))
    for total in range(2):
        for chunk in range(CHUNKS):
            for tag in range(2):
                for way in range(2):
                    names.append(("part", total, chunk, tag, way))
                    names.append(("pair", total, chunk, tag, way))
            names.append(("sum", total, chunk))
            names.append(("shift", total, chunk))
    names.append(("guest",))
    names.append(("leave",))
    return {name: number for number, name in enumerate(names)}


COPIES = copy_numbers()


def dot(left, right):
    return jnp.dot(left, right, preferred_element_type=F32)


def dot_last(left, right):
    return lax.dot_general(left, right, (((1,), (1,)), ((), ())), preferred_element_type=F32)


def dot_first(left, right):
    return lax.dot_general(left, right, (((0,), (0,)), ((), ())), preferred_element_type=F32)


def iota(shape, axis):
    return lax.broadcasted_iota(jnp.int32, shape, axis)


def relay_kernel(
    act_in,
    up_in,
    stash_in,
    guest_in,
    gain_in,
    query_in,
    keyval_in,
    output_in,
    marks_in,
    next_out,
    prev_out,
    held_out,
    kept_out,
    gath,
    part,
    halves,
    pairs,
    zsend,
    zrecv,
    act_v,
    stash_v,
    guest_v,
    back_v,
    gain_v,
    marks_v,
    kv_mixed,
    wcat,
    wout,
    qkv,
    context,
    gctx,
    gcat,
    pack_send,
    pack_recv,
    kept_v,
    held_v,
    shift_v,
    send_sem,
    recv_sem,
    local_sem,
):
    section = lax.axis_index("section")
    tensor = lax.axis_index("tensor")
    plane = tensor // 4
    y = tensor % 4
    sections = 32
    y_up = (y + 1) % 4
    y_down = (y + 3) % 4
    y_far = (y + 2) % 4

    def at(section_to, tensor_to):
        return {"section": section_to, "tensor": tensor_to}

    to_up = at(section, plane * 4 + y_up)
    to_down = at(section, plane * 4 + y_down)
    to_far_z = at(section, (1 - plane) * 4 + y)
    to_mirror = at(sections - 1 - section, tensor)
    to_next = at((section + 1) % sections, tensor)
    to_prev = at((section + sections - 1) % sections, tensor)
    peers = (to_up, to_down, to_far_z, to_mirror, to_next, to_prev)

    barrier = pltpu.get_barrier_semaphore()
    for peer in peers:
        pl.semaphore_signal(barrier, inc=1, device_id=peer, device_id_type=MESH)

    local = {}
    for number, (name, source, target) in enumerate(
        (
            ("up", up_in, gath.at[UP, plane, y]),
            ("act", act_in, act_v),
            ("gain", gain_in, gain_v),
            ("marks", marks_in, marks_v),
            ("guest", guest_in, guest_v),
            ("stash", stash_in, stash_v),
            ("keyval", keyval_in, kv_mixed),
            ("query", query_in, wcat.at[:, pl.ds(0, QCOLS)]),
            ("output", output_in, wout),
        )
    ):
        local[name] = pltpu.make_async_copy(source, target, local_sem.at[number])
        local[name].start()

    sends = []

    def remote(name, source, target, device):
        number = COPIES[name]
        return pltpu.make_async_remote_copy(
            src_ref=source,
            dst_ref=target,
            send_sem=send_sem.at[number],
            recv_sem=recv_sem.at[number],
            device_id=device,
            device_id_type=MESH,
        )

    def send(name, source, target, device):
        copy = remote(name, source, target, device)
        copy.start()
        sends.append(copy)

    def receive(name, target):
        remote(name, target, target, to_up).wait_recv()

    planes = (plane, 1 - plane)
    ways = ((to_up, y_down, 0), (to_down, y_up, HALF))

    def gather_z(which):
        ref = gath.at[which, plane, y]
        send(("z", which), ref, ref, to_far_z)

    def gather_z_done(which):
        receive(("z", which), gath.at[which, 1 - plane, y])

    def gather_y(which, tag):
        ref = gath.at[which, planes[tag], y]
        for way in range(2):
            send(("y", which, tag, way), ref, ref, ways[way][0])

    def gather_forward(which, tag):
        for way in range(2):
            target, source_y, column = ways[way]
            ref = gath.at[which, planes[tag], source_y]
            receive(("y", which, tag, way), ref)
            piece = ref.at[:, pl.ds(column, HALF)]
            send(("half", which, tag, way), piece, piece, target)

    def gather_done(which, tag):
        for way in range(2):
            column = ways[way][2]
            piece = gath.at[which, planes[tag], y_far, :, pl.ds(column, HALF)]
            receive(("half", which, tag, way), piece)

    def rows_of(chunk):
        return pl.ds(chunk * CHUNK, CHUNK)

    def sum_far(total, chunk, tag):
        for way in range(2):
            target, _, column = ways[way]
            piece = part.at[total, planes[tag], y_far, rows_of(chunk), pl.ds(column, HALF)]
            send(("part", total, chunk, tag, way), piece, halves.at[total, chunk, tag, way], target)

    def sum_near(total, chunk, tag):
        for way in range(2):
            target, _, column = ways[way]
            near = y_up if way == 0 else y_down
            landed = halves.at[total, chunk, tag, way]
            receive(("part", total, chunk, tag, way), landed)
            piece = (total, planes[tag], near, rows_of(chunk), pl.ds(column, HALF))
            part[piece] = (part[piece].astype(F32) + landed[...].astype(F32)).astype(BF16)
            send(
                ("pair", total, chunk, tag, way),
                part.at[total, planes[tag], near, rows_of(chunk)],
                pairs.at[total, chunk, tag, way],
                target,
            )

    def plane_sum(total, chunk, tag):
        for way in range(2):
            receive(("pair", total, chunk, tag, way), pairs.at[total, chunk, tag, way])
        own = part[total, planes[tag], y, rows_of(chunk)].astype(F32)
        return (
            own
            + pairs[total, chunk, tag, 0].astype(F32)
            + pairs[total, chunk, tag, 1].astype(F32)
        )

    def sum_cross(total, chunk):
        zsend[total, chunk] = plane_sum(total, chunk, 1).astype(BF16)
        send(("sum", total, chunk), zsend.at[total, chunk], zrecv.at[total, chunk], to_far_z)

    def sum_total(total, chunk):
        own = plane_sum(total, chunk, 0)
        receive(("sum", total, chunk), zrecv.at[total, chunk])
        return own + zrecv[total, chunk].astype(F32)

    def normed(values):
        factor = lax.rsqrt(jnp.mean(values * values, axis=-1, keepdims=True) + EPSILON)
        return (values * factor * gain_v[...]).astype(BF16)

    local["act"].wait()
    local["gain"].wait()
    gath[NOW, plane, y] = normed(act_v[...].astype(F32))
    local["up"].wait()
    pl.semaphore_wait(barrier, len(peers))
    gather_z(NOW)
    gather_y(UP, 0)
    gather_y(NOW, 0)

    local["marks"].wait()
    marked = jnp.where(marks_v[...] == 1, 1.0, 0.0).astype(BF16)
    spread = jnp.where(iota((ROWS, BLOCKS), 0) // 2 == iota((ROWS, BLOCKS), 1), 1.0, 0.0)
    row_marks = dot(spread.astype(BF16), marked)
    first = iota((ROWS, ROWS), 0)
    second = iota((ROWS, ROWS), 1)

    def selection(which_section):
        column = jnp.sum(jnp.where(second == which_section, row_marks, 0.0), axis=1, keepdims=True)
        wide = jnp.broadcast_to(column, (ROWS, ROWS))
        line = jnp.sum(jnp.where(first == second, wide, 0.0), axis=0, keepdims=True)
        line_rank = jnp.sum(jnp.where(first < second, wide, 0.0), axis=0, keepdims=True)
        tall = jnp.broadcast_to(line, (ROWS, ROWS))
        column_rank = jnp.sum(jnp.where(second < first, tall, 0.0), axis=1, keepdims=True)
        slot = iota((PACKED, ROWS), 0).astype(F32)
        pack = jnp.where(slot == line_rank, jnp.broadcast_to(line, (PACKED, ROWS)), 0.0)
        slot = iota((ROWS, PACKED), 1).astype(F32)
        unpack = jnp.where(slot == column_rank, jnp.broadcast_to(column, (ROWS, PACKED)), 0.0)
        return column > 0.5, pack.astype(BF16), unpack.astype(BF16)

    own_moved, own_pack, own_unpack = selection(section)
    far_moved, far_pack, far_unpack = selection(sections - 1 - section)
    local["guest"].wait()
    pack_send[0] = dot(far_pack, guest_v[...]).astype(BF16)
    send(("guest",), pack_send.at[0], pack_recv.at[0], to_mirror)
    gather_z(UP)
    pack_send[1] = dot(own_pack, act_v[...]).astype(BF16)
    send(("leave",), pack_send.at[1], pack_recv.at[1], to_mirror)
    kept_v[...] = jnp.where(own_moved, 0.0, act_v[...].astype(F32)).astype(BF16)
    kept_copy = pltpu.make_async_copy(kept_v, kept_out, local_sem.at[9])
    kept_copy.start()

    local["keyval"].wait()
    block = 2 * HEAD_DIM
    out_row = iota((block, block), 0)
    wanted = jnp.where(out_row < HEAD_DIM, 2 * out_row, 2 * (out_row - HEAD_DIM) + 1)
    sort_rows = jnp.where(iota((block, block), 1) == wanted, 1.0, 0.0).astype(BF16)

    def split_rows(step, carry):
        sorted_rows = dot(sort_rows, kv_mixed[pl.ds(pl.multiple_of(step * block, block), block), :])
        sorted_rows = sorted_rows.astype(BF16)
        target = pl.ds(pl.multiple_of(step * HEAD_DIM, HEAD_DIM), HEAD_DIM)
        wcat[target, QCOLS : QCOLS + HEAD_DIM] = sorted_rows[:HEAD_DIM]
        wcat[target, QCOLS + HEAD_DIM :] = sorted_rows[HEAD_DIM:]
        return carry

    lax.fori_loop(0, WIDTH // HEAD_DIM, split_rows, 0)

    gather_forward(UP, 0)
    local["stash"].wait()
    receive(("guest",), pack_recv.at[0])
    returned = dot(own_unpack, pack_recv[0])
    back_rows = jnp.where(own_moved, returned, stash_v[...].astype(F32))
    back_v[...] = back_rows.astype(BF16)
    gath[BACK, plane, y] = normed(back_rows)
    gather_y(BACK, 0)
    gather_z(BACK)
    gather_forward(NOW, 0)
    receive(("leave",), pack_recv.at[1])
    held_v[...] = dot(far_unpack, pack_recv[1]).astype(BF16)
    held_copy = pltpu.make_async_copy(held_v, held_out, local_sem.at[10])
    held_copy.start()
    gather_z_done(NOW)
    gather_y(NOW, 1)
    gather_forward(BACK, 0)
    gather_z_done(UP)
    gather_y(UP, 1)
    gather_forward(NOW, 1)
    gather_done(NOW, 0)
    gather_done(NOW, 1)
    local["query"].wait()

    def project(which):
        def tile(step, carry):
            columns = pl.ds(pl.multiple_of(step * 256, 256), 256)
            rows = gath[which].reshape(LENGTH, WIDTH)
            qkv[which // 2, :, columns] = dot(rows, wcat[:, columns]).astype(BF16)
            return carry

        lax.fori_loop(0, CCOLS // 256, tile, 0)

    scale = HEAD_DIM ** (-0.5)

    def probabilities(queries, keys):
        scores = dot_last(queries, keys) * scale
        allowed = iota((LENGTH, LENGTH), 0) >= iota((LENGTH, LENGTH), 1)
        masked = jnp.where(allowed, scores, NEG_LARGE)
        raised = jnp.exp(masked - jnp.max(masked, axis=-1, keepdims=True))
        return raised / jnp.sum(raised, axis=-1, keepdims=True)

    project(NOW)
    gather_z_done(BACK)
    gather_y(BACK, 1)
    gather_forward(UP, 1)

    keys_now = qkv[0, :, QCOLS : QCOLS + HEAD_DIM]
    values_now = qkv[0, :, QCOLS + HEAD_DIM :]
    for head in range(GROUP):
        columns = slice(head * HEAD_DIM, (head + 1) * HEAD_DIM)
        weights = probabilities(qkv[0, :, columns], keys_now).astype(BF16)
        context[:, columns] = dot(weights, values_now).astype(BF16)

    local["output"].wait()

    def forward_tile(step, carry):
        columns = pl.ds(pl.multiple_of(step * 512, 512), 512)
        result = dot(context[...], wout[:, columns]).astype(BF16)
        part[0, :, :, :, columns] = result.reshape(2, 4, ROWS, 512)
        return carry

    lax.fori_loop(0, WIDTH // 512, forward_tile, 0)

    gather_forward(BACK, 1)
    for chunk in range(CHUNKS):
        for tag in (1, 0):
            sum_far(0, chunk, tag)

    gather_done(UP, 0)
    gather_done(UP, 1)

    def grad_tile(step, carry):
        columns = pl.ds(pl.multiple_of(step * 256, 256), 256)
        rows = gath[UP].reshape(LENGTH, WIDTH)
        gctx[:, columns] = dot_last(rows, wout[columns, :]).astype(BF16)
        return carry

    lax.fori_loop(0, QCOLS // 256, grad_tile, 0)

    gather_done(BACK, 0)
    gather_done(BACK, 1)
    sum_near(0, 0, 1)
    sum_near(0, 0, 0)
    project(BACK)
    sum_near(0, 1, 1)
    sum_near(0, 1, 0)

    keys_back = qkv[1, :, QCOLS : QCOLS + HEAD_DIM]
    values_back = qkv[1, :, QCOLS + HEAD_DIM :]
    grad_key = jnp.zeros((LENGTH, HEAD_DIM), F32)
    grad_value = jnp.zeros((LENGTH, HEAD_DIM), F32)
    for head in range(GROUP):
        columns = slice(head * HEAD_DIM, (head + 1) * HEAD_DIM)
        queries = qkv[1, :, columns]
        grads = gctx[:, columns]
        probs = probabilities(queries, keys_back)
        grad_value = grad_value + dot_first(probs.astype(BF16), grads)
        grad_prob = dot_last(grads, values_back)
        inner = jnp.sum(probs * grad_prob, axis=-1, keepdims=True)
        grad_score = (probs * (grad_prob - inner) * scale).astype(BF16)
        gcat[:, columns] = dot(grad_score, keys_back).astype(BF16)
        grad_key = grad_key + dot_first(grad_score, queries)
    gcat[:, QCOLS : QCOLS + HEAD_DIM] = grad_key.astype(BF16)
    gcat[:, QCOLS + HEAD_DIM :] = grad_value.astype(BF16)

    sum_cross(0, 0)

    for chunk in range(CHUNKS):
        grads = gcat[...].reshape(8, ROWS, CCOLS)[:, chunk * CHUNK : (chunk + 1) * CHUNK]
        grads = grads.reshape(8 * CHUNK, CCOLS)

        def backward_tile(step, carry):
            columns = pl.ds(pl.multiple_of(step * 512, 512), 512)
            result = dot_last(grads, wcat[columns, :]).astype(BF16)
            part[1, :, :, rows_of(chunk), columns] = result.reshape(2, 4, CHUNK, 512)
            return carry

        lax.fori_loop(0, WIDTH // 512, backward_tile, 0)
        for tag in (1, 0):
            sum_far(1, chunk, tag)

    sum_cross(0, 1)

    def finish_forward(chunk):
        rows = rows_of(chunk)
        total = sum_total(0, chunk)
        shift_v[0, rows] = (act_v[rows, :].astype(F32) + total).astype(BF16)
        send(("shift", 0, chunk), shift_v.at[0, rows], next_out.at[rows], to_next)

    def finish_backward(chunk):
        rows = rows_of(chunk)
        values = back_v[rows, :].astype(F32)
        factor = lax.rsqrt(jnp.mean(values * values, axis=-1, keepdims=True) + EPSILON)
        upstream = gath[UP, plane, y, rows].astype(F32)
        grads = sum_total(1, chunk) * gain_v[...]
        inner = jnp.sum(grads * values, axis=-1, keepdims=True) * (factor * factor * factor)
        norm_grad = grads * factor - values * (inner * (1.0 / WIDTH))
        shift_v[1, rows] = (upstream + norm_grad).astype(BF16)
        send(("shift", 1, chunk), shift_v.at[1, rows], prev_out.at[rows], to_prev)

    sum_near(1, 0, 1)
    sum_near(1, 0, 0)
    finish_forward(0)
    sum_near(1, 1, 1)
    sum_near(1, 1, 0)
    finish_forward(1)
    sum_cross(1, 0)
    sum_cross(1, 1)
    finish_backward(0)
    finish_backward(1)

    kept_copy.wait()
    held_copy.wait()
    for copy in sends:
        copy.wait_send()
    for chunk in range(CHUNKS):
        receive(("shift", 0, chunk), next_out.at[rows_of(chunk)])
        receive(("shift", 1, chunk), prev_out.at[rows_of(chunk)])


def relay(act, up, stash, guest, gain, query, keyval, output, marks):
    block = jax.ShapeDtypeStruct((ROWS, WIDTH), BF16)
    anywhere = pl.BlockSpec(memory_space=pl.ANY)
    count = len(COPIES)
    vmem = pltpu.VMEM
    return pl.pallas_call(
        relay_kernel,
        out_shape=(block, block, block, block),
        in_specs=[anywhere] * 9,
        out_specs=(anywhere,) * 4,
        scratch_shapes=[
            vmem((3, 2, 4, ROWS, WIDTH), BF16),
            vmem((2, 2, 4, ROWS, WIDTH), BF16),
            vmem((2, CHUNKS, 2, 2, CHUNK, HALF), BF16),
            vmem((2, CHUNKS, 2, 2, CHUNK, WIDTH), BF16),
            vmem((2, CHUNKS, CHUNK, WIDTH), BF16),
            vmem((2, CHUNKS, CHUNK, WIDTH), BF16),
            vmem((ROWS, WIDTH), BF16),
            vmem((ROWS, WIDTH), BF16),
            vmem((ROWS, WIDTH), BF16),
            vmem((ROWS, WIDTH), BF16),
            vmem((1, WIDTH), F32),
            vmem((BLOCKS, 32), jnp.int32),
            vmem((2 * WIDTH, HEAD_DIM), BF16),
            vmem((WIDTH, CCOLS), BF16),
            vmem((QCOLS, WIDTH), BF16),
            vmem((2, LENGTH, CCOLS), BF16),
            vmem((LENGTH, QCOLS), BF16),
            vmem((LENGTH, QCOLS), BF16),
            vmem((LENGTH, CCOLS), BF16),
            vmem((2, PACKED, WIDTH), BF16),
            vmem((2, PACKED, WIDTH), BF16),
            vmem((ROWS, WIDTH), BF16),
            vmem((ROWS, WIDTH), BF16),
            vmem((2, ROWS, WIDTH), BF16),
            pltpu.SemaphoreType.DMA((count,)),
            pltpu.SemaphoreType.DMA((count,)),
            pltpu.SemaphoreType.DMA((11,)),
        ],
        compiler_params=pltpu.CompilerParams(
            collective_id=0, has_side_effects=True, vmem_limit_bytes=60 * 2**20
        ),
    )(act, up, stash, guest, gain, query, keyval, output, marks)


def local(
    activations,
    upstream_grad,
    stash_blocks,
    guest_blocks,
    norm_gain,
    query_weight,
    keyval_weight,
    output_weight,
    evict_marks,
):
    section = lax.axis_index("section")
    next_raw, prev_raw, held, kept = relay(
        activations[0],
        upstream_grad[0],
        stash_blocks[0],
        guest_blocks[0],
        norm_gain,
        query_weight[0],
        keyval_weight[0].reshape(2 * WIDTH, HEAD_DIM),
        output_weight[0],
        evict_marks.T,
    )
    next_input = jnp.where(section == 0, jnp.zeros_like(next_raw), next_raw)
    last = lax.axis_size("section") - 1
    prev_grad = jnp.where(section == last, jnp.zeros_like(prev_raw), prev_raw)
    return (next_input[None], prev_grad[None], kept[None], held[None])


def solution(mesh):
    placed = (
        P("section", "tensor", None),
        P("section", "tensor", None),
        P("section", "tensor", None),
        P("section", "tensor", None),
        P("section", None),
        P("section", None, "tensor"),
        P("section", None, None, "tensor"),
        P("section", "tensor", None),
        P(),
    )
    return jax.shard_map(
        local,
        mesh=mesh,
        in_specs=placed,
        out_specs=(P("section", "tensor", None),) * 4,
        check_vma=False,
    )
```

```python
import jax
import jax.numpy as jnp
from jax import lax
from jax.experimental import pallas as pl
from jax.experimental.pallas import tpu as pltpu
from jax.sharding import PartitionSpec as P

HEADS = 32
KV_HEADS = 8
HEAD_DIM = 128
GROUP = HEADS // KV_HEADS
EPSILON = 1e-05
NEG_LARGE = -1e30
MESH = pl.DeviceIdType.MESH
F32 = jnp.float32
BF16 = jnp.bfloat16

ROWS = 32
WIDTH = 4096
HALF = WIDTH // 2
QUARTER = WIDTH // 4
BLOCKS = 16
PACKED = 16
CHUNKS = 4
CHUNK = ROWS // CHUNKS
STAGES = 2
QCOLS = 512
CCOLS = 768
LENGTH = 256
NOW, UP, BACK = 0, 1, 2


def copy_numbers():
    names = []
    for tensor in range(3):
        for way in range(2):
            names.append(("own", tensor, way))
            names.append(("own half", tensor, way))
        for piece in range(2):
            names.append(("z", tensor, piece))
            for way in range(2):
                names.append(("far", tensor, piece, way))
                names.append(("far half", tensor, piece, way))
    for total in range(2):
        for chunk in range(CHUNKS):
            for tag in range(2):
                for way in range(2):
                    names.append(("part", total, chunk, tag, way))
                    names.append(("pair", total, chunk, tag, way))
            names.append(("sum", total, chunk))
            names.append(("shift", total, chunk))
    names.append(("guest",))
    names.append(("leave",))
    return {name: number for number, name in enumerate(names)}


COPIES = copy_numbers()


def dot(left, right):
    return jnp.dot(left, right, preferred_element_type=F32)


def dot_last(left, right):
    return lax.dot_general(left, right, (((1,), (1,)), ((), ())), preferred_element_type=F32)


def dot_first(left, right):
    return lax.dot_general(left, right, (((0,), (0,)), ((), ())), preferred_element_type=F32)


def iota(shape, axis):
    return lax.broadcasted_iota(jnp.int32, shape, axis)


def relay_kernel(
    act_in,
    up_in,
    stash_in,
    guest_in,
    gain_in,
    query_in,
    keyval_in,
    output_in,
    marks_in,
    next_out,
    prev_out,
    held_out,
    kept_out,
    gath,
    part,
    halves,
    pairs,
    zsend,
    zrecv,
    act_v,
    stash_v,
    guest_v,
    back_v,
    gain_v,
    marks_v,
    kv_mixed,
    wcat,
    wout,
    qkv,
    context,
    gctx,
    gcat,
    pack_send,
    pack_recv,
    kept_v,
    held_v,
    shift_v,
    send_sem,
    recv_sem,
    local_sem,
):
    section = lax.axis_index("section")
    tensor = lax.axis_index("tensor")
    plane = tensor // 4
    y = tensor % 4
    sections = 32
    y_up = (y + 1) % 4
    y_down = (y + 3) % 4
    y_far = (y + 2) % 4

    def at(section_to, tensor_to):
        return {"section": section_to, "tensor": tensor_to}

    to_up = at(section, plane * 4 + y_up)
    to_down = at(section, plane * 4 + y_down)
    to_far_z = at(section, (1 - plane) * 4 + y)
    to_mirror = at(sections - 1 - section, tensor)
    to_next = at((section + 1) % sections, tensor)
    to_prev = at((section + sections - 1) % sections, tensor)
    peers = (to_up, to_down, to_far_z, to_mirror, to_next, to_prev)

    barrier = pltpu.get_barrier_semaphore()
    for peer in peers:
        pl.semaphore_signal(barrier, inc=1, device_id=peer, device_id_type=MESH)

    local = {}
    for number, (name, source, target) in enumerate(
        (
            ("up", up_in, gath.at[UP, plane, y]),
            ("act", act_in, act_v),
            ("gain", gain_in, gain_v),
            ("marks", marks_in, marks_v),
            ("guest", guest_in, guest_v),
            ("stash", stash_in, stash_v),
            ("keyval", keyval_in, kv_mixed),
            ("query", query_in, wcat.at[:, pl.ds(0, QCOLS)]),
            ("output", output_in, wout),
        )
    ):
        local[name] = pltpu.make_async_copy(source, target, local_sem.at[number])
        local[name].start()

    sends = []

    def remote(name, source, target, device):
        number = COPIES[name]
        return pltpu.make_async_remote_copy(
            src_ref=source,
            dst_ref=target,
            send_sem=send_sem.at[number],
            recv_sem=recv_sem.at[number],
            device_id=device,
            device_id_type=MESH,
        )

    def send(name, source, target, device):
        copy = remote(name, source, target, device)
        copy.start()
        sends.append(copy)

    def receive(name, target):
        remote(name, target, target, to_up).wait_recv()

    planes = (plane, 1 - plane)
    ways = ((to_up, y_down, 0), (to_down, y_up, HALF))

    def columns_of(piece):
        return pl.ds(piece * HALF, HALF)

    def cross(which, piece):
        ref = gath.at[which, plane, y, :, columns_of(piece)]
        send(("z", which, piece), ref, ref, to_far_z)

    def crossed(which, piece):
        receive(("z", which, piece), gath.at[which, 1 - plane, y, :, columns_of(piece)])
        ref = gath.at[which, 1 - plane, y, :, columns_of(piece)]
        for way in range(2):
            send(("far", which, piece, way), ref, ref, ways[way][0])

    def far_forward(which, piece):
        for way in range(2):
            target, source_y, _ = ways[way]
            ref = gath.at[which, 1 - plane, source_y]
            receive(("far", which, piece, way), ref.at[:, columns_of(piece)])
            part_ref = ref.at[:, pl.ds(piece * HALF + way * QUARTER, QUARTER)]
            send(("far half", which, piece, way), part_ref, part_ref, target)

    def far_done(which):
        for piece in range(2):
            for way in range(2):
                columns = pl.ds(piece * HALF + way * QUARTER, QUARTER)
                receive(
                    ("far half", which, piece, way), gath.at[which, 1 - plane, y_far, :, columns]
                )

    def own_send(which):
        ref = gath.at[which, plane, y]
        for way in range(2):
            send(("own", which, way), ref, ref, ways[way][0])

    def own_forward(which):
        for way in range(2):
            target, source_y, column = ways[way]
            ref = gath.at[which, plane, source_y]
            receive(("own", which, way), ref)
            piece = ref.at[:, pl.ds(column, HALF)]
            send(("own half", which, way), piece, piece, target)

    def own_done(which):
        for way in range(2):
            piece = gath.at[which, plane, y_far, :, pl.ds(ways[way][2], HALF)]
            receive(("own half", which, way), piece)

    def rows_of(chunk):
        return pl.ds(chunk * CHUNK, CHUNK)

    def sum_far(total, chunk, tag):
        for way in range(2):
            target, _, column = ways[way]
            piece = part.at[total, planes[tag], y_far, chunk, :, pl.ds(column, HALF)]
            send(("part", total, chunk, tag, way), piece, halves.at[total, chunk, tag, way], target)

    def sum_near(total, chunk, tag):
        for way in range(2):
            target, _, column = ways[way]
            near = y_up if way == 0 else y_down
            landed = halves.at[total, chunk, tag, way]
            receive(("part", total, chunk, tag, way), landed)
            piece = (total, planes[tag], near, chunk, slice(None), pl.ds(column, HALF))
            part[piece] = (part[piece].astype(F32) + landed[...].astype(F32)).astype(BF16)
            send(
                ("pair", total, chunk, tag, way),
                part.at[total, planes[tag], near, chunk],
                pairs.at[total, chunk, tag, way],
                target,
            )

    def near(total, chunk):
        sum_near(total, chunk, 1)
        sum_near(total, chunk, 0)

    def plane_sum(total, chunk, tag):
        for way in range(2):
            receive(("pair", total, chunk, tag, way), pairs.at[total, chunk, tag, way])
        own = part[total, planes[tag], y, chunk].astype(F32)
        return (
            own
            + pairs[total, chunk, tag, 0].astype(F32)
            + pairs[total, chunk, tag, 1].astype(F32)
        )

    def sum_cross(total, chunk):
        zsend[total, chunk] = plane_sum(total, chunk, 1).astype(BF16)
        send(("sum", total, chunk), zsend.at[total, chunk], zrecv.at[total, chunk], to_far_z)

    def sum_total(total, chunk):
        own = plane_sum(total, chunk, 0)
        receive(("sum", total, chunk), zrecv.at[total, chunk])
        return own + zrecv[total, chunk].astype(F32)

    def normed(values):
        factor = lax.rsqrt(jnp.mean(values * values, axis=-1, keepdims=True) + EPSILON)
        return (values * factor * gain_v[...]).astype(BF16)

    local["marks"].wait()
    marked = jnp.where(marks_v[...] == 1, 1.0, 0.0).astype(BF16)
    spread = jnp.where(iota((ROWS, BLOCKS), 0) // 2 == iota((ROWS, BLOCKS), 1), 1.0, 0.0)
    row_marks = dot(spread.astype(BF16), marked)
    first = iota((ROWS, ROWS), 0)
    second = iota((ROWS, ROWS), 1)

    def selection(which_section):
        column = jnp.sum(jnp.where(second == which_section, row_marks, 0.0), axis=1, keepdims=True)
        wide = jnp.broadcast_to(column, (ROWS, ROWS))
        line = jnp.sum(jnp.where(first == second, wide, 0.0), axis=0, keepdims=True)
        line_rank = jnp.sum(jnp.where(first < second, wide, 0.0), axis=0, keepdims=True)
        tall = jnp.broadcast_to(line, (ROWS, ROWS))
        column_rank = jnp.sum(jnp.where(second < first, tall, 0.0), axis=1, keepdims=True)
        slot = iota((PACKED, ROWS), 0).astype(F32)
        pack = jnp.where(slot == line_rank, jnp.broadcast_to(line, (PACKED, ROWS)), 0.0)
        slot = iota((ROWS, PACKED), 1).astype(F32)
        unpack = jnp.where(slot == column_rank, jnp.broadcast_to(column, (ROWS, PACKED)), 0.0)
        return column > 0.5, pack.astype(BF16), unpack.astype(BF16)

    own_moved, own_pack, own_unpack = selection(section)
    far_moved, far_pack, far_unpack = selection(sections - 1 - section)
    local["guest"].wait()
    pack_send[0] = dot(far_pack, guest_v[...]).astype(BF16)
    local["act"].wait()
    local["gain"].wait()
    gath[NOW, plane, y] = normed(act_v[...].astype(F32))
    local["up"].wait()
    pl.semaphore_wait(barrier, len(peers))
    send(("guest",), pack_send.at[0], pack_recv.at[0], to_mirror)
    own_send(UP)
    own_send(NOW)
    pack_send[1] = dot(own_pack, act_v[...]).astype(BF16)
    kept_v[...] = jnp.where(own_moved, 0.0, act_v[...].astype(F32)).astype(BF16)
    kept_copy = pltpu.make_async_copy(kept_v, kept_out, local_sem.at[9])
    kept_copy.start()

    local["keyval"].wait()
    block = 2 * HEAD_DIM
    out_row = iota((block, block), 0)
    wanted = jnp.where(out_row < HEAD_DIM, 2 * out_row, 2 * (out_row - HEAD_DIM) + 1)
    sort_rows = jnp.where(iota((block, block), 1) == wanted, 1.0, 0.0).astype(BF16)

    def split_rows(step, carry):
        sorted_rows = dot(sort_rows, kv_mixed[pl.ds(pl.multiple_of(step * block, block), block), :])
        sorted_rows = sorted_rows.astype(BF16)
        target = pl.ds(pl.multiple_of(step * HEAD_DIM, HEAD_DIM), HEAD_DIM)
        wcat[target, QCOLS : QCOLS + HEAD_DIM] = sorted_rows[:HEAD_DIM]
        wcat[target, QCOLS + HEAD_DIM :] = sorted_rows[HEAD_DIM:]
        return carry

    lax.fori_loop(0, WIDTH // HEAD_DIM, split_rows, 0)

    own_forward(UP)
    receive(("guest",), pack_recv.at[0])
    cross(NOW, 0)
    cross(NOW, 1)
    local["stash"].wait()
    returned = dot(own_unpack, pack_recv[0])
    back_rows = jnp.where(own_moved, returned, stash_v[...].astype(F32))
    back_v[...] = back_rows.astype(BF16)
    gath[BACK, plane, y] = normed(back_rows)
    own_send(BACK)
    own_forward(NOW)
    crossed(NOW, 0)
    cross(BACK, 0)
    crossed(NOW, 1)
    cross(BACK, 1)
    own_forward(BACK)
    far_forward(NOW, 0)
    far_forward(NOW, 1)
    crossed(BACK, 0)
    cross(UP, 0)
    crossed(BACK, 1)
    cross(UP, 1)
    own_done(UP)
    own_done(NOW)
    far_done(NOW)
    local["query"].wait()

    def project(which):
        def tile(step, carry):
            columns = pl.ds(pl.multiple_of(step * 256, 256), 256)
            rows = gath[which].reshape(LENGTH, WIDTH)
            qkv[which // 2, :, columns] = dot(rows, wcat[:, columns]).astype(BF16)
            return carry

        lax.fori_loop(0, CCOLS // 256, tile, 0)

    scale = HEAD_DIM ** (-0.5)

    def probabilities(queries, keys):
        scores = dot_last(queries, keys) * scale
        allowed = iota((LENGTH, LENGTH), 0) >= iota((LENGTH, LENGTH), 1)
        masked = jnp.where(allowed, scores, NEG_LARGE)
        raised = jnp.exp(masked - jnp.max(masked, axis=-1, keepdims=True))
        return raised / jnp.sum(raised, axis=-1, keepdims=True)

    project(NOW)
    far_forward(BACK, 0)
    far_forward(BACK, 1)
    crossed(UP, 0)

    keys_now = qkv[0, :, QCOLS : QCOLS + HEAD_DIM]
    values_now = qkv[0, :, QCOLS + HEAD_DIM :]
    for head in range(GROUP):
        columns = slice(head * HEAD_DIM, (head + 1) * HEAD_DIM)
        weights = probabilities(qkv[0, :, columns], keys_now).astype(BF16)
        context[:, columns] = dot(weights, values_now).astype(BF16)

    crossed(UP, 1)
    send(("leave",), pack_send.at[1], pack_recv.at[1], to_mirror)
    local["output"].wait()

    def forward_tile(step, carry):
        columns = pl.ds(pl.multiple_of(step * 512, 512), 512)
        result = dot(context[...], wout[:, columns]).reshape(2, 4, CHUNKS, CHUNK, 512)
        part[0, :, :, :, :, columns] = result.astype(BF16)
        return carry

    lax.fori_loop(0, WIDTH // 512, forward_tile, 0)

    for chunk in range(CHUNKS):
        for tag in (1, 0):
            sum_far(0, chunk, tag)
    far_forward(UP, 0)
    far_forward(UP, 1)
    own_done(BACK)
    far_done(BACK)
    project(BACK)
    for chunk in range(CHUNKS):
        near(0, chunk)
    far_done(UP)

    def grad_tile(step, carry):
        columns = pl.ds(pl.multiple_of(step * 256, 256), 256)
        rows = gath[UP].reshape(LENGTH, WIDTH)
        gctx[:, columns] = dot_last(rows, wout[columns, :]).astype(BF16)
        return carry

    lax.fori_loop(0, QCOLS // 256, grad_tile, 0)

    keys_back = qkv[1, :, QCOLS : QCOLS + HEAD_DIM]
    values_back = qkv[1, :, QCOLS + HEAD_DIM :]
    grad_key = jnp.zeros((LENGTH, HEAD_DIM), F32)
    grad_value = jnp.zeros((LENGTH, HEAD_DIM), F32)
    for head in range(GROUP):
        columns = slice(head * HEAD_DIM, (head + 1) * HEAD_DIM)
        queries = qkv[1, :, columns]
        grads = gctx[:, columns]
        probs = probabilities(queries, keys_back)
        grad_value = grad_value + dot_first(probs.astype(BF16), grads)
        grad_prob = dot_last(grads, values_back)
        inner = jnp.sum(probs * grad_prob, axis=-1, keepdims=True)
        grad_score = (probs * (grad_prob - inner) * scale).astype(BF16)
        gcat[:, columns] = dot(grad_score, keys_back).astype(BF16)
        grad_key = grad_key + dot_first(grad_score, queries)
    gcat[:, QCOLS : QCOLS + HEAD_DIM] = grad_key.astype(BF16)
    gcat[:, QCOLS + HEAD_DIM :] = grad_value.astype(BF16)

    receive(("leave",), pack_recv.at[1])
    held_v[...] = dot(far_unpack, pack_recv[1]).astype(BF16)
    held_copy = pltpu.make_async_copy(held_v, held_out, local_sem.at[10])
    held_copy.start()
    sum_cross(0, 0)
    sum_cross(0, 1)

    stage_rows = ROWS // STAGES
    stage_chunks = CHUNKS // STAGES
    for stage in range(STAGES):
        grads = gcat[...].reshape(8, ROWS, CCOLS)[:, stage * stage_rows : (stage + 1) * stage_rows]
        grads = grads.reshape(8 * stage_rows, CCOLS)

        stage_chunk = pl.ds(stage * stage_chunks, stage_chunks)

        def backward_tile(step, carry):
            columns = pl.ds(pl.multiple_of(step * 512, 512), 512)
            result = dot_last(grads, wcat[columns, :]).reshape(2, 4, stage_chunks, CHUNK, 512)
            part[1, :, :, stage_chunk, :, columns] = result.astype(BF16)
            return carry

        lax.fori_loop(0, WIDTH // 512, backward_tile, 0)
        for chunk in range(stage * stage_chunks, (stage + 1) * stage_chunks):
            for tag in (1, 0):
                sum_far(1, chunk, tag)

    sum_cross(0, 2)
    sum_cross(0, 3)

    def finish_forward(chunk):
        rows = rows_of(chunk)
        total = sum_total(0, chunk)
        shift_v[0, chunk] = (act_v[rows, :].astype(F32) + total).astype(BF16)
        send(("shift", 0, chunk), shift_v.at[0, chunk], next_out.at[rows], to_next)

    def finish_backward(chunk):
        rows = rows_of(chunk)
        values = back_v[rows, :].astype(F32)
        factor = lax.rsqrt(jnp.mean(values * values, axis=-1, keepdims=True) + EPSILON)
        upstream = gath[UP, plane, y, rows].astype(F32)
        grads = sum_total(1, chunk) * gain_v[...]
        inner = jnp.sum(grads * values, axis=-1, keepdims=True) * (factor * factor * factor)
        norm_grad = grads * factor - values * (inner * (1.0 / WIDTH))
        shift_v[1, chunk] = (upstream + norm_grad).astype(BF16)
        send(("shift", 1, chunk), shift_v.at[1, chunk], prev_out.at[rows], to_prev)

    for chunk in range(CHUNKS):
        near(1, chunk)
    for chunk in range(CHUNKS):
        finish_forward(chunk)
    for chunk in range(CHUNKS):
        sum_cross(1, chunk)
        if chunk > 0:
            finish_backward(chunk - 1)
    finish_backward(CHUNKS - 1)

    kept_copy.wait()
    held_copy.wait()
    for copy in sends:
        copy.wait_send()
    for chunk in range(CHUNKS):
        receive(("shift", 0, chunk), next_out.at[rows_of(chunk)])
        receive(("shift", 1, chunk), prev_out.at[rows_of(chunk)])


def relay(act, up, stash, guest, gain, query, keyval, output, marks):
    block = jax.ShapeDtypeStruct((ROWS, WIDTH), BF16)
    anywhere = pl.BlockSpec(memory_space=pl.ANY)
    count = len(COPIES)
    vmem = pltpu.VMEM
    return pl.pallas_call(
        relay_kernel,
        out_shape=(block, block, block, block),
        in_specs=[anywhere] * 9,
        out_specs=(anywhere,) * 4,
        scratch_shapes=[
            vmem((3, 2, 4, ROWS, WIDTH), BF16),
            vmem((2, 2, 4, CHUNKS, CHUNK, WIDTH), BF16),
            vmem((2, CHUNKS, 2, 2, CHUNK, HALF), BF16),
            vmem((2, CHUNKS, 2, 2, CHUNK, WIDTH), BF16),
            vmem((2, CHUNKS, CHUNK, WIDTH), BF16),
            vmem((2, CHUNKS, CHUNK, WIDTH), BF16),
            vmem((ROWS, WIDTH), BF16),
            vmem((ROWS, WIDTH), BF16),
            vmem((ROWS, WIDTH), BF16),
            vmem((ROWS, WIDTH), BF16),
            vmem((1, WIDTH), F32),
            vmem((BLOCKS, 32), jnp.int32),
            vmem((2 * WIDTH, HEAD_DIM), BF16),
            vmem((WIDTH, CCOLS), BF16),
            vmem((QCOLS, WIDTH), BF16),
            vmem((2, LENGTH, CCOLS), BF16),
            vmem((LENGTH, QCOLS), BF16),
            vmem((LENGTH, QCOLS), BF16),
            vmem((LENGTH, CCOLS), BF16),
            vmem((2, PACKED, WIDTH), BF16),
            vmem((2, PACKED, WIDTH), BF16),
            vmem((ROWS, WIDTH), BF16),
            vmem((ROWS, WIDTH), BF16),
            vmem((2, CHUNKS, CHUNK, WIDTH), BF16),
            pltpu.SemaphoreType.DMA((count,)),
            pltpu.SemaphoreType.DMA((count,)),
            pltpu.SemaphoreType.DMA((11,)),
        ],
        compiler_params=pltpu.CompilerParams(
            collective_id=0, has_side_effects=True, vmem_limit_bytes=60 * 2**20
        ),
    )(act, up, stash, guest, gain, query, keyval, output, marks)


def local(
    activations,
    upstream_grad,
    stash_blocks,
    guest_blocks,
    norm_gain,
    query_weight,
    keyval_weight,
    output_weight,
    evict_marks,
):
    section = lax.axis_index("section")
    next_raw, prev_raw, held, kept = relay(
        activations[0],
        upstream_grad[0],
        stash_blocks[0],
        guest_blocks[0],
        norm_gain,
        query_weight[0],
        keyval_weight[0].reshape(2 * WIDTH, HEAD_DIM),
        output_weight[0],
        evict_marks.T,
    )
    last = lax.axis_size("section") - 1

    def unless(empty, rows):
        return jnp.where(empty, jnp.zeros_like(rows), rows)[None]

    return (
        unless(section == 0, next_raw),
        unless(section == last, prev_raw),
        unless(section > last, kept),
        unless(section > last, held),
    )


def solution(mesh):
    placed = (
        P("section", "tensor", None),
        P("section", "tensor", None),
        P("section", "tensor", None),
        P("section", "tensor", None),
        P("section", None),
        P("section", None, "tensor"),
        P("section", None, None, "tensor"),
        P("section", "tensor", None),
        P(),
    )
    return jax.shard_map(
        local,
        mesh=mesh,
        in_specs=placed,
        out_specs=(P("section", "tensor", None),) * 4,
        check_vma=False,
    )
```

```python
import jax
import jax.numpy as jnp
from jax import lax
from jax.experimental import pallas as pl
from jax.experimental.pallas import tpu as pltpu
from jax.sharding import PartitionSpec as P

HEADS = 32
KV_HEADS = 8
HEAD_DIM = 128
GROUP = HEADS // KV_HEADS
EPSILON = 1e-05
NEG_LARGE = -1e30
MESH = pl.DeviceIdType.MESH
F32 = jnp.float32
BF16 = jnp.bfloat16

ROWS = 32
WIDTH = 4096
HALF = WIDTH // 2
PIECE = ROWS // 2
BLOCKS = 16
PACKED = 16
CHUNKS = 4
CHUNK = ROWS // CHUNKS
STAGES = 2
QCOLS = 512
CCOLS = 768
LENGTH = 256
NOW, UP, BACK = 0, 1, 2


def copy_numbers():
    names = []
    for tensor in range(3):
        for way in range(2):
            names.append(("own", tensor, way))
            names.append(("own half", tensor, way))
        for piece in range(2):
            names.append(("z", tensor, piece))
            for way in range(2):
                names.append(("far", tensor, piece, way))
                names.append(("far half", tensor, piece, way))
    for total in range(2):
        for chunk in range(CHUNKS):
            for tag in range(2):
                for way in range(2):
                    names.append(("part", total, chunk, tag, way))
                    names.append(("pair", total, chunk, tag, way))
            if total == 0:
                names.append(("sum", total, chunk))
            names.append(("shift", total, chunk))
    for chunk in range(CHUNKS):
        names.append(("shift far", chunk))
    names.append(("guest",))
    names.append(("leave",))
    return {name: number for number, name in enumerate(names)}


COPIES = copy_numbers()


def dot(left, right):
    return jnp.dot(left, right, preferred_element_type=F32)


def dot_last(left, right):
    return lax.dot_general(left, right, (((1,), (1,)), ((), ())), preferred_element_type=F32)


def dot_first(left, right):
    return lax.dot_general(left, right, (((0,), (0,)), ((), ())), preferred_element_type=F32)


def iota(shape, axis):
    return lax.broadcasted_iota(jnp.int32, shape, axis)


def relay_kernel(
    act_in,
    up_in,
    stash_in,
    guest_in,
    gain_in,
    query_in,
    keyval_in,
    output_in,
    marks_in,
    next_out,
    prev_out,
    prev_far_out,
    held_out,
    kept_out,
    gath,
    part,
    halves,
    pairs,
    zsend,
    zrecv,
    act_v,
    stash_v,
    guest_v,
    back_v,
    far_back_v,
    gain_v,
    marks_v,
    kv_mixed,
    wcat,
    wout,
    qkv,
    context,
    gctx,
    gcat,
    pack_send,
    pack_recv,
    kept_v,
    held_v,
    shift_v,
    send_sem,
    recv_sem,
    local_sem,
):
    section = lax.axis_index("section")
    tensor = lax.axis_index("tensor")
    plane = tensor // 4
    y = tensor % 4
    sections = 32
    y_up = (y + 1) % 4
    y_down = (y + 3) % 4
    y_far = (y + 2) % 4

    def at(section_to, tensor_to):
        return {"section": section_to, "tensor": tensor_to}

    to_up = at(section, plane * 4 + y_up)
    to_down = at(section, plane * 4 + y_down)
    to_far_z = at(section, (1 - plane) * 4 + y)
    to_mirror = at(sections - 1 - section, tensor)
    to_next = at((section + 1) % sections, tensor)
    to_prev = at((section + sections - 1) % sections, tensor)
    to_prev_far = at((section + sections - 1) % sections, (1 - plane) * 4 + y)
    from_next_far = at((section + 1) % sections, (1 - plane) * 4 + y)
    peers = (to_up, to_down, to_far_z, to_mirror, to_next, to_prev, to_prev_far, from_next_far)

    barrier = pltpu.get_barrier_semaphore()
    for peer in peers:
        pl.semaphore_signal(barrier, inc=1, device_id=peer, device_id_type=MESH)

    local = {}
    for number, (name, source, target) in enumerate(
        (
            ("up", up_in, gath.at[UP, plane, y]),
            ("act", act_in, act_v),
            ("gain", gain_in, gain_v),
            ("marks", marks_in, marks_v),
            ("guest", guest_in, guest_v),
            ("stash", stash_in, stash_v),
            ("keyval", keyval_in, kv_mixed),
            ("query", query_in, wcat.at[:, pl.ds(0, QCOLS)]),
            ("output", output_in, wout),
        )
    ):
        local[name] = pltpu.make_async_copy(source, target, local_sem.at[number])
        local[name].start()

    sends = []

    def remote(name, source, target, device):
        number = COPIES[name]
        return pltpu.make_async_remote_copy(
            src_ref=source,
            dst_ref=target,
            send_sem=send_sem.at[number],
            recv_sem=recv_sem.at[number],
            device_id=device,
            device_id_type=MESH,
        )

    def send(name, source, target, device):
        copy = remote(name, source, target, device)
        copy.start()
        sends.append(copy)

    def receive(name, target):
        remote(name, target, target, to_up).wait_recv()

    planes = (plane, 1 - plane)
    ways = ((to_up, y_down, 0), (to_down, y_up, HALF))

    def piece_rows(piece):
        return pl.ds(piece * PIECE, PIECE)

    def cross(which, piece):
        rows = piece_rows(piece)
        if which == BACK:
            source, target = back_v.at[rows], far_back_v.at[rows]
        else:
            source = gath.at[which, plane, y, rows]
            target = source
        send(("z", which, piece), source, target, to_far_z)

    def crossed(which, piece):
        rows = piece_rows(piece)
        ref = gath.at[which, 1 - plane, y, rows]
        if which == BACK:
            receive(("z", which, piece), far_back_v.at[rows])
            gath[which, 1 - plane, y, rows] = normed(far_back_v[rows, :].astype(F32))
        else:
            receive(("z", which, piece), ref)
        for way in range(2):
            send(("far", which, piece, way), ref, ref, ways[way][0])

    def far_forward(which, piece):
        for way in range(2):
            target, source_y, column = ways[way]
            ref = gath.at[which, 1 - plane, source_y, piece_rows(piece)]
            receive(("far", which, piece, way), ref)
            part_ref = ref.at[:, pl.ds(column, HALF)]
            send(("far half", which, piece, way), part_ref, part_ref, target)

    def far_done(which):
        for piece in range(2):
            for way in range(2):
                columns = pl.ds(ways[way][2], HALF)
                ref = gath.at[which, 1 - plane, y_far, piece_rows(piece), columns]
                receive(("far half", which, piece, way), ref)

    def own_send(which):
        ref = gath.at[which, plane, y]
        for way in range(2):
            send(("own", which, way), ref, ref, ways[way][0])

    def own_forward(which):
        for way in range(2):
            target, source_y, column = ways[way]
            ref = gath.at[which, plane, source_y]
            receive(("own", which, way), ref)
            piece = ref.at[:, pl.ds(column, HALF)]
            send(("own half", which, way), piece, piece, target)

    def own_done(which):
        for way in range(2):
            piece = gath.at[which, plane, y_far, :, pl.ds(ways[way][2], HALF)]
            receive(("own half", which, way), piece)

    def rows_of(chunk):
        return pl.ds(chunk * CHUNK, CHUNK)

    def sum_far(total, chunk, tag):
        for way in range(2):
            target, _, column = ways[way]
            piece = part.at[total, planes[tag], y_far, chunk, :, pl.ds(column, HALF)]
            send(("part", total, chunk, tag, way), piece, halves.at[total, chunk, tag, way], target)

    def sum_near(total, chunk, tag):
        for way in range(2):
            target, _, column = ways[way]
            near = y_up if way == 0 else y_down
            landed = halves.at[total, chunk, tag, way]
            receive(("part", total, chunk, tag, way), landed)
            piece = (total, planes[tag], near, chunk, slice(None), pl.ds(column, HALF))
            part[piece] = (part[piece].astype(F32) + landed[...].astype(F32)).astype(BF16)
            send(
                ("pair", total, chunk, tag, way),
                part.at[total, planes[tag], near, chunk],
                pairs.at[total, chunk, tag, way],
                target,
            )

    def near(total, chunk):
        sum_near(total, chunk, 1)
        sum_near(total, chunk, 0)

    def plane_sum(total, chunk, tag):
        for way in range(2):
            receive(("pair", total, chunk, tag, way), pairs.at[total, chunk, tag, way])
        own = part[total, planes[tag], y, chunk].astype(F32)
        return (
            own
            + pairs[total, chunk, tag, 0].astype(F32)
            + pairs[total, chunk, tag, 1].astype(F32)
        )

    def sum_cross(total, chunk):
        zsend[total, chunk] = plane_sum(total, chunk, 1).astype(BF16)
        send(("sum", total, chunk), zsend.at[total, chunk], zrecv.at[total, chunk], to_far_z)

    def sum_total(total, chunk):
        own = plane_sum(total, chunk, 0)
        receive(("sum", total, chunk), zrecv.at[total, chunk])
        return own + zrecv[total, chunk].astype(F32)

    def normed(values):
        factor = lax.rsqrt(jnp.mean(values * values, axis=-1, keepdims=True) + EPSILON)
        return (values * factor * gain_v[...]).astype(BF16)

    local["marks"].wait()
    marked = jnp.where(marks_v[...] == 1, 1.0, 0.0).astype(BF16)
    spread = jnp.where(iota((ROWS, BLOCKS), 0) // 2 == iota((ROWS, BLOCKS), 1), 1.0, 0.0)
    row_marks = dot(spread.astype(BF16), marked)
    first = iota((ROWS, ROWS), 0)
    second = iota((ROWS, ROWS), 1)

    def selection(which_section):
        column = jnp.sum(jnp.where(second == which_section, row_marks, 0.0), axis=1, keepdims=True)
        wide = jnp.broadcast_to(column, (ROWS, ROWS))
        line = jnp.sum(jnp.where(first == second, wide, 0.0), axis=0, keepdims=True)
        line_rank = jnp.sum(jnp.where(first < second, wide, 0.0), axis=0, keepdims=True)
        tall = jnp.broadcast_to(line, (ROWS, ROWS))
        column_rank = jnp.sum(jnp.where(second < first, tall, 0.0), axis=1, keepdims=True)
        slot = iota((PACKED, ROWS), 0).astype(F32)
        pack = jnp.where(slot == line_rank, jnp.broadcast_to(line, (PACKED, ROWS)), 0.0)
        slot = iota((ROWS, PACKED), 1).astype(F32)
        unpack = jnp.where(slot == column_rank, jnp.broadcast_to(column, (ROWS, PACKED)), 0.0)
        return column > 0.5, pack.astype(BF16), unpack.astype(BF16)

    own_moved, own_pack, own_unpack = selection(section)
    far_moved, far_pack, far_unpack = selection(sections - 1 - section)
    local["guest"].wait()
    pack_send[0] = dot(far_pack, guest_v[...]).astype(BF16)
    local["act"].wait()
    local["gain"].wait()
    gath[NOW, plane, y] = normed(act_v[...].astype(F32))
    local["up"].wait()
    pl.semaphore_wait(barrier, len(peers))
    send(("guest",), pack_send.at[0], pack_recv.at[0], to_mirror)
    own_send(UP)
    own_send(NOW)
    pack_send[1] = dot(own_pack, act_v[...]).astype(BF16)
    kept_v[...] = jnp.where(own_moved, 0.0, act_v[...].astype(F32)).astype(BF16)
    kept_copy = pltpu.make_async_copy(kept_v, kept_out, local_sem.at[9])
    kept_copy.start()

    local["keyval"].wait()
    block = 2 * HEAD_DIM
    out_row = iota((block, block), 0)
    wanted = jnp.where(out_row < HEAD_DIM, 2 * out_row, 2 * (out_row - HEAD_DIM) + 1)
    sort_rows = jnp.where(iota((block, block), 1) == wanted, 1.0, 0.0).astype(BF16)

    def split_rows(step, carry):
        sorted_rows = dot(sort_rows, kv_mixed[pl.ds(pl.multiple_of(step * block, block), block), :])
        sorted_rows = sorted_rows.astype(BF16)
        target = pl.ds(pl.multiple_of(step * HEAD_DIM, HEAD_DIM), HEAD_DIM)
        wcat[target, QCOLS : QCOLS + HEAD_DIM] = sorted_rows[:HEAD_DIM]
        wcat[target, QCOLS + HEAD_DIM :] = sorted_rows[HEAD_DIM:]
        return carry

    lax.fori_loop(0, WIDTH // HEAD_DIM, split_rows, 0)

    own_forward(UP)
    receive(("guest",), pack_recv.at[0])
    cross(NOW, 0)
    cross(NOW, 1)
    local["stash"].wait()
    returned = dot(own_unpack, pack_recv[0])
    back_rows = jnp.where(own_moved, returned, stash_v[...].astype(F32))
    back_v[...] = back_rows.astype(BF16)
    gath[BACK, plane, y] = normed(back_rows)
    own_send(BACK)
    own_forward(NOW)
    crossed(NOW, 0)
    cross(BACK, 0)
    crossed(NOW, 1)
    cross(BACK, 1)
    own_forward(BACK)
    far_forward(NOW, 0)
    far_forward(NOW, 1)
    crossed(BACK, 0)
    cross(UP, 0)
    crossed(BACK, 1)
    cross(UP, 1)
    own_done(UP)
    own_done(NOW)
    far_done(NOW)
    local["query"].wait()

    def project(which):
        def tile(step, carry):
            columns = pl.ds(pl.multiple_of(step * 256, 256), 256)
            rows = gath[which].reshape(LENGTH, WIDTH)
            qkv[which // 2, :, columns] = dot(rows, wcat[:, columns]).astype(BF16)
            return carry

        lax.fori_loop(0, CCOLS // 256, tile, 0)

    scale = HEAD_DIM ** (-0.5)

    def probabilities(queries, keys):
        scores = dot_last(queries, keys) * scale
        allowed = iota((LENGTH, LENGTH), 0) >= iota((LENGTH, LENGTH), 1)
        masked = jnp.where(allowed, scores, NEG_LARGE)
        raised = jnp.exp(masked - jnp.max(masked, axis=-1, keepdims=True))
        return raised / jnp.sum(raised, axis=-1, keepdims=True)

    project(NOW)
    far_forward(BACK, 0)
    far_forward(BACK, 1)
    crossed(UP, 0)

    keys_now = qkv[0, :, QCOLS : QCOLS + HEAD_DIM]
    values_now = qkv[0, :, QCOLS + HEAD_DIM :]
    for head in range(GROUP):
        columns = slice(head * HEAD_DIM, (head + 1) * HEAD_DIM)
        weights = probabilities(qkv[0, :, columns], keys_now).astype(BF16)
        context[:, columns] = dot(weights, values_now).astype(BF16)

    crossed(UP, 1)
    send(("leave",), pack_send.at[1], pack_recv.at[1], to_mirror)
    local["output"].wait()

    def forward_tile(step, carry):
        columns = pl.ds(pl.multiple_of(step * 512, 512), 512)
        result = dot(context[...], wout[:, columns]).reshape(2, 4, CHUNKS, CHUNK, 512)
        part[0, :, :, :, :, columns] = result.astype(BF16)
        return carry

    lax.fori_loop(0, WIDTH // 512, forward_tile, 0)

    for chunk in range(CHUNKS):
        for tag in (1, 0):
            sum_far(0, chunk, tag)
    far_forward(UP, 0)
    far_forward(UP, 1)
    own_done(BACK)
    far_done(BACK)
    project(BACK)
    for chunk in range(CHUNKS):
        near(0, chunk)
    far_done(UP)

    def grad_tile(step, carry):
        columns = pl.ds(pl.multiple_of(step * 256, 256), 256)
        rows = gath[UP].reshape(LENGTH, WIDTH)
        gctx[:, columns] = dot_last(rows, wout[columns, :]).astype(BF16)
        return carry

    lax.fori_loop(0, QCOLS // 256, grad_tile, 0)

    keys_back = qkv[1, :, QCOLS : QCOLS + HEAD_DIM]
    values_back = qkv[1, :, QCOLS + HEAD_DIM :]
    grad_key = jnp.zeros((LENGTH, HEAD_DIM), F32)
    grad_value = jnp.zeros((LENGTH, HEAD_DIM), F32)
    for head in range(GROUP):
        columns = slice(head * HEAD_DIM, (head + 1) * HEAD_DIM)
        queries = qkv[1, :, columns]
        grads = gctx[:, columns]
        probs = probabilities(queries, keys_back)
        grad_value = grad_value + dot_first(probs.astype(BF16), grads)
        grad_prob = dot_last(grads, values_back)
        inner = jnp.sum(probs * grad_prob, axis=-1, keepdims=True)
        grad_score = (probs * (grad_prob - inner) * scale).astype(BF16)
        gcat[:, columns] = dot(grad_score, keys_back).astype(BF16)
        grad_key = grad_key + dot_first(grad_score, queries)
    gcat[:, QCOLS : QCOLS + HEAD_DIM] = grad_key.astype(BF16)
    gcat[:, QCOLS + HEAD_DIM :] = grad_value.astype(BF16)

    receive(("leave",), pack_recv.at[1])
    held_v[...] = dot(far_unpack, pack_recv[1]).astype(BF16)
    held_copy = pltpu.make_async_copy(held_v, held_out, local_sem.at[10])
    held_copy.start()
    sum_cross(0, 0)
    sum_cross(0, 1)

    stage_rows = ROWS // STAGES
    stage_chunks = CHUNKS // STAGES
    for stage in range(STAGES):
        grads = gcat[...].reshape(8, ROWS, CCOLS)[:, stage * stage_rows : (stage + 1) * stage_rows]
        grads = grads.reshape(8 * stage_rows, CCOLS)

        stage_chunk = pl.ds(stage * stage_chunks, stage_chunks)

        def backward_tile(step, carry):
            columns = pl.ds(pl.multiple_of(step * 512, 512), 512)
            result = dot_last(grads, wcat[columns, :]).reshape(2, 4, stage_chunks, CHUNK, 512)
            part[1, :, :, stage_chunk, :, columns] = result.astype(BF16)
            return carry

        lax.fori_loop(0, WIDTH // 512, backward_tile, 0)
        for chunk in range(stage * stage_chunks, (stage + 1) * stage_chunks):
            for tag in (1, 0):
                sum_far(1, chunk, tag)

    sum_cross(0, 2)
    sum_cross(0, 3)

    def finish_forward(chunk):
        rows = rows_of(chunk)
        total = sum_total(0, chunk)
        shift_v[0, chunk] = (act_v[rows, :].astype(F32) + total).astype(BF16)
        send(("shift", 0, chunk), shift_v.at[0, chunk], next_out.at[rows], to_next)

    def norm_grad(values, total):
        factor = lax.rsqrt(jnp.mean(values * values, axis=-1, keepdims=True) + EPSILON)
        grads = total * gain_v[...]
        inner = jnp.sum(grads * values, axis=-1, keepdims=True) * (factor * factor * factor)
        return grads * factor - values * (inner * (1.0 / WIDTH))

    def finish_far(chunk):
        rows = rows_of(chunk)
        grad = norm_grad(far_back_v[rows, :].astype(F32), plane_sum(1, chunk, 1))
        zsend[1, chunk] = grad.astype(BF16)
        send(("shift far", chunk), zsend.at[1, chunk], prev_far_out.at[rows], to_prev_far)

    def finish_own(chunk):
        rows = rows_of(chunk)
        grad = norm_grad(back_v[rows, :].astype(F32), plane_sum(1, chunk, 0))
        upstream = gath[UP, plane, y, rows].astype(F32)
        shift_v[1, chunk] = (upstream + grad).astype(BF16)
        send(("shift", 1, chunk), shift_v.at[1, chunk], prev_out.at[rows], to_prev)

    for tag in (1, 0):
        for chunk in range(CHUNKS):
            sum_near(1, chunk, tag)
    for chunk in range(CHUNKS):
        finish_forward(chunk)
    for chunk in range(CHUNKS):
        finish_far(chunk)
    for chunk in range(CHUNKS):
        finish_own(chunk)

    kept_copy.wait()
    held_copy.wait()
    for copy in sends:
        copy.wait_send()
    for chunk in range(CHUNKS):
        receive(("shift", 0, chunk), next_out.at[rows_of(chunk)])
        receive(("shift", 1, chunk), prev_out.at[rows_of(chunk)])
        receive(("shift far", chunk), prev_far_out.at[rows_of(chunk)])


def relay(act, up, stash, guest, gain, query, keyval, output, marks):
    block = jax.ShapeDtypeStruct((ROWS, WIDTH), BF16)
    anywhere = pl.BlockSpec(memory_space=pl.ANY)
    count = len(COPIES)
    vmem = pltpu.VMEM
    return pl.pallas_call(
        relay_kernel,
        out_shape=(block,) * 5,
        in_specs=[anywhere] * 9,
        out_specs=(anywhere,) * 5,
        scratch_shapes=[
            vmem((3, 2, 4, ROWS, WIDTH), BF16),
            vmem((2, 2, 4, CHUNKS, CHUNK, WIDTH), BF16),
            vmem((2, CHUNKS, 2, 2, CHUNK, HALF), BF16),
            vmem((2, CHUNKS, 2, 2, CHUNK, WIDTH), BF16),
            vmem((2, CHUNKS, CHUNK, WIDTH), BF16),
            vmem((2, CHUNKS, CHUNK, WIDTH), BF16),
            vmem((ROWS, WIDTH), BF16),
            vmem((ROWS, WIDTH), BF16),
            vmem((ROWS, WIDTH), BF16),
            vmem((ROWS, WIDTH), BF16),
            vmem((ROWS, WIDTH), BF16),
            vmem((1, WIDTH), F32),
            vmem((BLOCKS, 32), jnp.int32),
            vmem((2 * WIDTH, HEAD_DIM), BF16),
            vmem((WIDTH, CCOLS), BF16),
            vmem((QCOLS, WIDTH), BF16),
            vmem((2, LENGTH, CCOLS), BF16),
            vmem((LENGTH, QCOLS), BF16),
            vmem((LENGTH, QCOLS), BF16),
            vmem((LENGTH, CCOLS), BF16),
            vmem((2, PACKED, WIDTH), BF16),
            vmem((2, PACKED, WIDTH), BF16),
            vmem((ROWS, WIDTH), BF16),
            vmem((ROWS, WIDTH), BF16),
            vmem((2, CHUNKS, CHUNK, WIDTH), BF16),
            pltpu.SemaphoreType.DMA((count,)),
            pltpu.SemaphoreType.DMA((count,)),
            pltpu.SemaphoreType.DMA((11,)),
        ],
        compiler_params=pltpu.CompilerParams(
            collective_id=0, has_side_effects=True, vmem_limit_bytes=60 * 2**20
        ),
    )(act, up, stash, guest, gain, query, keyval, output, marks)


def finish_kernel(
    next_in,
    prev_in,
    prev_far_in,
    held_in,
    kept_in,
    next_out,
    prev_out,
    kept_out,
    held_out,
    next_v,
    prev_v,
    prev_far_v,
    held_v,
    kept_v,
    sem,
):
    section = lax.axis_index("section")
    arrivals = (
        (next_in, next_v),
        (prev_in, prev_v),
        (prev_far_in, prev_far_v),
        (held_in, held_v),
        (kept_in, kept_v),
    )
    loads = []
    for number, (source, target) in enumerate(arrivals):
        loads.append(pltpu.make_async_copy(source, target, sem.at[number]))
        loads[-1].start()
    stores = []

    def store(source, target):
        stores.append(pltpu.make_async_copy(source, target, sem.at[5 + len(stores)]))
        stores[-1].start()

    loads[0].wait()
    next_v[...] = jnp.where(section == 0, 0.0, next_v[...].astype(F32)).astype(BF16)
    store(next_v, next_out)
    loads[1].wait()
    loads[2].wait()
    total = prev_v[...].astype(F32) + prev_far_v[...].astype(F32)
    prev_v[...] = jnp.where(section == 31, 0.0, total).astype(BF16)
    store(prev_v, prev_out)
    loads[3].wait()
    store(held_v, held_out)
    loads[4].wait()
    store(kept_v, kept_out)
    for copy in stores:
        copy.wait()


def finish(*raw):
    block = jax.ShapeDtypeStruct((ROWS, WIDTH), BF16)
    anywhere = pl.BlockSpec(memory_space=pl.ANY)
    return pl.pallas_call(
        finish_kernel,
        out_shape=(block,) * 4,
        in_specs=[anywhere] * 5,
        out_specs=(anywhere,) * 4,
        scratch_shapes=[pltpu.VMEM((ROWS, WIDTH), BF16)] * 5 + [pltpu.SemaphoreType.DMA((9,))],
        compiler_params=pltpu.CompilerParams(vmem_limit_bytes=60 * 2**20),
    )(*raw)


def local(
    activations,
    upstream_grad,
    stash_blocks,
    guest_blocks,
    norm_gain,
    query_weight,
    keyval_weight,
    output_weight,
    evict_marks,
):
    raw = relay(
        activations[0],
        upstream_grad[0],
        stash_blocks[0],
        guest_blocks[0],
        norm_gain,
        query_weight[0],
        keyval_weight[0].reshape(2 * WIDTH, HEAD_DIM),
        output_weight[0],
        evict_marks.T,
    )
    return tuple(rows[None] for rows in finish(*raw))


def solution(mesh):
    placed = (
        P("section", "tensor", None),
        P("section", "tensor", None),
        P("section", "tensor", None),
        P("section", "tensor", None),
        P("section", None),
        P("section", None, "tensor"),
        P("section", None, None, "tensor"),
        P("section", "tensor", None),
        P(),
    )
    return jax.shard_map(
        local,
        mesh=mesh,
        in_specs=placed,
        out_specs=(P("section", "tensor", None),) * 4,
        check_vma=False,
    )
```

```python
import jax
import jax.numpy as jnp
from jax import lax
from jax.experimental import pallas as pl
from jax.experimental.pallas import tpu as pltpu
from jax.sharding import PartitionSpec as P

HEADS = 32
KV_HEADS = 8
HEAD_DIM = 128
GROUP = HEADS // KV_HEADS
EPSILON = 1e-05
NEG_LARGE = -1e30
MESH = pl.DeviceIdType.MESH
F32 = jnp.float32
BF16 = jnp.bfloat16

ROWS = 32
WIDTH = 4096
HALF = WIDTH // 2
PIECE = ROWS // 2
BLOCKS = 16
PACKED = 16
CHUNKS = 4
CHUNK = ROWS // CHUNKS
STAGES = 2
QCOLS = 512
CCOLS = 768
LENGTH = 256
NOW, UP, BACK = 0, 1, 2


def copy_numbers():
    names = []
    for tensor in range(3):
        for way in range(2):
            names.append(("own", tensor, way))
            names.append(("own half", tensor, way))
        for piece in range(2):
            names.append(("z", tensor, piece))
            for way in range(2):
                names.append(("far", tensor, piece, way))
                names.append(("far half", tensor, piece, way))
    for total in range(2):
        for chunk in range(CHUNKS):
            for tag in range(2):
                for way in range(2):
                    names.append(("part", total, chunk, tag, way))
                    names.append(("pair", total, chunk, tag, way))
            if total == 0:
                names.append(("sum", total, chunk))
            names.append(("shift", total, chunk))
    for chunk in range(CHUNKS):
        names.append(("shift far", chunk))
    names.append(("guest",))
    names.append(("leave",))
    return {name: number for number, name in enumerate(names)}


COPIES = copy_numbers()


def dot(left, right):
    return jnp.dot(left, right, preferred_element_type=F32)


def dot_last(left, right):
    return lax.dot_general(left, right, (((1,), (1,)), ((), ())), preferred_element_type=F32)


def dot_first(left, right):
    return lax.dot_general(left, right, (((0,), (0,)), ((), ())), preferred_element_type=F32)


def iota(shape, axis):
    return lax.broadcasted_iota(jnp.int32, shape, axis)


def relay_kernel(
    act_in,
    up_in,
    stash_in,
    guest_in,
    gain_in,
    query_in,
    keyval_in,
    output_in,
    marks_in,
    next_out,
    prev_out,
    prev_far_out,
    held_out,
    kept_out,
    gath,
    part,
    halves,
    pairs,
    zsend,
    zrecv,
    act_v,
    stash_v,
    guest_v,
    back_v,
    far_back_v,
    gain_v,
    marks_v,
    kv_mixed,
    wcat,
    wout,
    qkv,
    context,
    gctx,
    gcat,
    pack_send,
    pack_recv,
    kept_v,
    held_v,
    shift_v,
    send_sem,
    recv_sem,
    local_sem,
):
    section = lax.axis_index("section")
    tensor = lax.axis_index("tensor")
    plane = tensor // 4
    y = tensor % 4
    sections = 32
    y_up = (y + 1) % 4
    y_down = (y + 3) % 4
    y_far = (y + 2) % 4

    def at(section_to, tensor_to):
        return {"section": section_to, "tensor": tensor_to}

    to_up = at(section, plane * 4 + y_up)
    to_down = at(section, plane * 4 + y_down)
    to_far_z = at(section, (1 - plane) * 4 + y)
    to_mirror = at(sections - 1 - section, tensor)
    to_next = at((section + 1) % sections, tensor)
    to_prev = at((section + sections - 1) % sections, tensor)
    to_prev_far = at((section + sections - 1) % sections, (1 - plane) * 4 + y)
    from_next_far = at((section + 1) % sections, (1 - plane) * 4 + y)
    peers = (to_up, to_down, to_far_z, to_mirror, to_next, to_prev, to_prev_far, from_next_far)

    barrier = pltpu.get_barrier_semaphore()
    for peer in peers:
        pl.semaphore_signal(barrier, inc=1, device_id=peer, device_id_type=MESH)

    local = {}
    for number, (name, source, target) in enumerate(
        (
            ("up", up_in, gath.at[UP, plane, y]),
            ("act", act_in, act_v),
            ("gain", gain_in, gain_v),
            ("marks", marks_in, marks_v),
            ("guest", guest_in, guest_v),
            ("stash", stash_in, stash_v),
            ("keyval", keyval_in, kv_mixed),
            ("query", query_in, wcat.at[:, pl.ds(0, QCOLS)]),
            ("output", output_in, wout),
        )
    ):
        local[name] = pltpu.make_async_copy(source, target, local_sem.at[number])
        local[name].start()

    sends = []

    def remote(name, source, target, device):
        number = COPIES[name]
        return pltpu.make_async_remote_copy(
            src_ref=source,
            dst_ref=target,
            send_sem=send_sem.at[number],
            recv_sem=recv_sem.at[number],
            device_id=device,
            device_id_type=MESH,
        )

    def send(name, source, target, device):
        copy = remote(name, source, target, device)
        copy.start()
        sends.append(copy)

    def receive(name, target):
        remote(name, target, target, to_up).wait_recv()

    planes = (plane, 1 - plane)
    ways = ((to_up, y_down, 0), (to_down, y_up, HALF))

    def piece_rows(piece):
        return pl.ds(piece * PIECE, PIECE)

    def cross(which, piece):
        rows = piece_rows(piece)
        if which == BACK:
            source, target = back_v.at[rows], far_back_v.at[rows]
        else:
            source = gath.at[which, plane, y, rows]
            target = source
        send(("z", which, piece), source, target, to_far_z)

    def crossed(which, piece):
        rows = piece_rows(piece)
        ref = gath.at[which, 1 - plane, y, rows]
        if which == BACK:
            receive(("z", which, piece), far_back_v.at[rows])
            gath[which, 1 - plane, y, rows] = normed(far_back_v[rows, :].astype(F32))
        else:
            receive(("z", which, piece), ref)
        for way in range(2):
            send(("far", which, piece, way), ref, ref, ways[way][0])

    def far_forward(which, piece):
        for way in range(2):
            target, source_y, column = ways[way]
            ref = gath.at[which, 1 - plane, source_y, piece_rows(piece)]
            receive(("far", which, piece, way), ref)
            part_ref = ref.at[:, pl.ds(column, HALF)]
            send(("far half", which, piece, way), part_ref, part_ref, target)

    def far_done(which):
        for piece in range(2):
            for way in range(2):
                columns = pl.ds(ways[way][2], HALF)
                ref = gath.at[which, 1 - plane, y_far, piece_rows(piece), columns]
                receive(("far half", which, piece, way), ref)

    def own_send(which):
        ref = gath.at[which, plane, y]
        for way in range(2):
            send(("own", which, way), ref, ref, ways[way][0])

    def own_forward(which):
        for way in range(2):
            target, source_y, column = ways[way]
            ref = gath.at[which, plane, source_y]
            receive(("own", which, way), ref)
            piece = ref.at[:, pl.ds(column, HALF)]
            send(("own half", which, way), piece, piece, target)

    def own_done(which):
        for way in range(2):
            piece = gath.at[which, plane, y_far, :, pl.ds(ways[way][2], HALF)]
            receive(("own half", which, way), piece)

    def rows_of(chunk):
        return pl.ds(chunk * CHUNK, CHUNK)

    def sum_far(total, chunk, tag):
        for way in range(2):
            target, _, column = ways[way]
            piece = part.at[total, planes[tag], y_far, chunk, :, pl.ds(column, HALF)]
            send(("part", total, chunk, tag, way), piece, halves.at[total, chunk, tag, way], target)

    def sum_near(total, chunk, tag):
        for way in range(2):
            target, _, column = ways[way]
            near = y_up if way == 0 else y_down
            landed = halves.at[total, chunk, tag, way]
            receive(("part", total, chunk, tag, way), landed)
            piece = (total, planes[tag], near, chunk, slice(None), pl.ds(column, HALF))
            part[piece] = (part[piece].astype(F32) + landed[...].astype(F32)).astype(BF16)
            send(
                ("pair", total, chunk, tag, way),
                part.at[total, planes[tag], near, chunk],
                pairs.at[total, chunk, tag, way],
                target,
            )

    def near(total, chunk):
        sum_near(total, chunk, 1)
        sum_near(total, chunk, 0)

    def plane_sum(total, chunk, tag):
        for way in range(2):
            receive(("pair", total, chunk, tag, way), pairs.at[total, chunk, tag, way])
        own = part[total, planes[tag], y, chunk].astype(F32)
        return (
            own
            + pairs[total, chunk, tag, 0].astype(F32)
            + pairs[total, chunk, tag, 1].astype(F32)
        )

    def sum_cross(total, chunk):
        zsend[total, chunk] = plane_sum(total, chunk, 1).astype(BF16)
        send(("sum", total, chunk), zsend.at[total, chunk], zrecv.at[total, chunk], to_far_z)

    def sum_total(total, chunk):
        own = plane_sum(total, chunk, 0)
        receive(("sum", total, chunk), zrecv.at[total, chunk])
        return own + zrecv[total, chunk].astype(F32)

    def normed(values):
        factor = lax.rsqrt(jnp.mean(values * values, axis=-1, keepdims=True) + EPSILON)
        return (values * factor * gain_v[...]).astype(BF16)

    local["marks"].wait()
    marked = jnp.where(marks_v[...] == 1, 1.0, 0.0).astype(BF16)
    spread = jnp.where(iota((ROWS, BLOCKS), 0) // 2 == iota((ROWS, BLOCKS), 1), 1.0, 0.0)
    row_marks = dot(spread.astype(BF16), marked)
    first = iota((ROWS, ROWS), 0)
    second = iota((ROWS, ROWS), 1)

    def selection(which_section):
        column = jnp.sum(jnp.where(second == which_section, row_marks, 0.0), axis=1, keepdims=True)
        wide = jnp.broadcast_to(column, (ROWS, ROWS))
        line = jnp.sum(jnp.where(first == second, wide, 0.0), axis=0, keepdims=True)
        line_rank = jnp.sum(jnp.where(first < second, wide, 0.0), axis=0, keepdims=True)
        tall = jnp.broadcast_to(line, (ROWS, ROWS))
        column_rank = jnp.sum(jnp.where(second < first, tall, 0.0), axis=1, keepdims=True)
        slot = iota((PACKED, ROWS), 0).astype(F32)
        pack = jnp.where(slot == line_rank, jnp.broadcast_to(line, (PACKED, ROWS)), 0.0)
        slot = iota((ROWS, PACKED), 1).astype(F32)
        unpack = jnp.where(slot == column_rank, jnp.broadcast_to(column, (ROWS, PACKED)), 0.0)
        return column > 0.5, pack.astype(BF16), unpack.astype(BF16)

    own_moved, own_pack, own_unpack = selection(section)
    far_moved, far_pack, far_unpack = selection(sections - 1 - section)
    local["guest"].wait()
    pack_send[0] = dot(far_pack, guest_v[...]).astype(BF16)
    local["act"].wait()
    local["gain"].wait()
    gath[NOW, plane, y] = normed(act_v[...].astype(F32))
    local["up"].wait()
    pl.semaphore_wait(barrier, len(peers))
    send(("guest",), pack_send.at[0], pack_recv.at[0], to_mirror)
    own_send(UP)
    own_send(NOW)
    pack_send[1] = dot(own_pack, act_v[...]).astype(BF16)
    kept_v[...] = jnp.where(own_moved, 0.0, act_v[...].astype(F32)).astype(BF16)
    kept_copy = pltpu.make_async_copy(kept_v, kept_out, local_sem.at[9])
    kept_copy.start()

    local["keyval"].wait()
    block = 2 * HEAD_DIM
    out_row = iota((block, block), 0)
    wanted = jnp.where(out_row < HEAD_DIM, 2 * out_row, 2 * (out_row - HEAD_DIM) + 1)
    sort_rows = jnp.where(iota((block, block), 1) == wanted, 1.0, 0.0).astype(BF16)

    def split_rows(step, carry):
        sorted_rows = dot(sort_rows, kv_mixed[pl.ds(pl.multiple_of(step * block, block), block), :])
        sorted_rows = sorted_rows.astype(BF16)
        target = pl.ds(pl.multiple_of(step * HEAD_DIM, HEAD_DIM), HEAD_DIM)
        wcat[target, QCOLS : QCOLS + HEAD_DIM] = sorted_rows[:HEAD_DIM]
        wcat[target, QCOLS + HEAD_DIM :] = sorted_rows[HEAD_DIM:]
        return carry

    lax.fori_loop(0, WIDTH // HEAD_DIM, split_rows, 0)

    own_forward(UP)
    receive(("guest",), pack_recv.at[0])
    cross(NOW, 0)
    cross(NOW, 1)
    local["stash"].wait()
    returned = dot(own_unpack, pack_recv[0])
    back_rows = jnp.where(own_moved, returned, stash_v[...].astype(F32))
    back_v[...] = back_rows.astype(BF16)
    gath[BACK, plane, y] = normed(back_rows)
    own_send(BACK)
    own_forward(NOW)
    crossed(NOW, 0)
    cross(BACK, 0)
    crossed(NOW, 1)
    cross(BACK, 1)
    own_forward(BACK)
    far_forward(NOW, 0)
    far_forward(NOW, 1)
    crossed(BACK, 0)
    cross(UP, 0)
    crossed(BACK, 1)
    cross(UP, 1)
    own_done(UP)
    own_done(NOW)
    far_done(NOW)
    local["query"].wait()

    def project(which):
        def tile(step, carry):
            columns = pl.ds(pl.multiple_of(step * 256, 256), 256)
            rows = gath[which].reshape(LENGTH, WIDTH)
            qkv[which // 2, :, columns] = dot(rows, wcat[:, columns]).astype(BF16)
            return carry

        lax.fori_loop(0, CCOLS // 256, tile, 0)

    scale = HEAD_DIM ** (-0.5)

    def probabilities(queries, keys):
        scores = dot_last(queries, keys) * scale
        allowed = iota((LENGTH, LENGTH), 0) >= iota((LENGTH, LENGTH), 1)
        masked = jnp.where(allowed, scores, NEG_LARGE)
        raised = jnp.exp(masked - jnp.max(masked, axis=-1, keepdims=True))
        return raised / jnp.sum(raised, axis=-1, keepdims=True)

    project(NOW)
    far_forward(BACK, 0)
    far_forward(BACK, 1)
    crossed(UP, 0)

    keys_now = qkv[0, :, QCOLS : QCOLS + HEAD_DIM]
    values_now = qkv[0, :, QCOLS + HEAD_DIM :]
    for head in range(GROUP):
        columns = slice(head * HEAD_DIM, (head + 1) * HEAD_DIM)
        weights = probabilities(qkv[0, :, columns], keys_now).astype(BF16)
        context[:, columns] = dot(weights, values_now).astype(BF16)

    crossed(UP, 1)
    send(("leave",), pack_send.at[1], pack_recv.at[1], to_mirror)
    local["output"].wait()

    def forward_tile(step, carry):
        columns = pl.ds(pl.multiple_of(step * 512, 512), 512)
        result = dot(context[...], wout[:, columns]).reshape(2, 4, CHUNKS, CHUNK, 512)
        part[0, :, :, :, :, columns] = result.astype(BF16)
        return carry

    lax.fori_loop(0, WIDTH // 512, forward_tile, 0)

    for chunk in range(CHUNKS):
        for tag in (1, 0):
            sum_far(0, chunk, tag)
    far_forward(UP, 0)
    far_forward(UP, 1)
    own_done(BACK)
    far_done(BACK)
    project(BACK)
    for chunk in range(CHUNKS):
        near(0, chunk)
    far_done(UP)

    def grad_tile(step, carry):
        columns = pl.ds(pl.multiple_of(step * 256, 256), 256)
        rows = gath[UP].reshape(LENGTH, WIDTH)
        gctx[:, columns] = dot_last(rows, wout[columns, :]).astype(BF16)
        return carry

    lax.fori_loop(0, QCOLS // 256, grad_tile, 0)

    keys_back = qkv[1, :, QCOLS : QCOLS + HEAD_DIM]
    values_back = qkv[1, :, QCOLS + HEAD_DIM :]
    grad_key = jnp.zeros((LENGTH, HEAD_DIM), F32)
    grad_value = jnp.zeros((LENGTH, HEAD_DIM), F32)
    for head in range(GROUP):
        columns = slice(head * HEAD_DIM, (head + 1) * HEAD_DIM)
        queries = qkv[1, :, columns]
        grads = gctx[:, columns]
        probs = probabilities(queries, keys_back)
        grad_value = grad_value + dot_first(probs.astype(BF16), grads)
        grad_prob = dot_last(grads, values_back)
        inner = jnp.sum(probs * grad_prob, axis=-1, keepdims=True)
        grad_score = (probs * (grad_prob - inner) * scale).astype(BF16)
        gcat[:, columns] = dot(grad_score, keys_back).astype(BF16)
        grad_key = grad_key + dot_first(grad_score, queries)
    gcat[:, QCOLS : QCOLS + HEAD_DIM] = grad_key.astype(BF16)
    gcat[:, QCOLS + HEAD_DIM :] = grad_value.astype(BF16)

    receive(("leave",), pack_recv.at[1])
    held_v[...] = dot(far_unpack, pack_recv[1]).astype(BF16)
    held_copy = pltpu.make_async_copy(held_v, held_out, local_sem.at[10])
    held_copy.start()
    sum_cross(0, 0)
    sum_cross(0, 1)

    stage_rows = ROWS // STAGES
    stage_chunks = CHUNKS // STAGES
    for stage in range(STAGES):
        grads = gcat[...].reshape(8, ROWS, CCOLS)[:, stage * stage_rows : (stage + 1) * stage_rows]
        grads = grads.reshape(8 * stage_rows, CCOLS)

        stage_chunk = pl.ds(stage * stage_chunks, stage_chunks)

        def backward_tile(step, carry):
            columns = pl.ds(pl.multiple_of(step * 512, 512), 512)
            result = dot_last(grads, wcat[columns, :]).reshape(2, 4, stage_chunks, CHUNK, 512)
            part[1, :, :, stage_chunk, :, columns] = result.astype(BF16)
            return carry

        lax.fori_loop(0, WIDTH // 512, backward_tile, 0)
        for tag in (1, 0):
            for chunk in range(stage * stage_chunks, (stage + 1) * stage_chunks):
                sum_far(1, chunk, tag)

    sum_cross(0, 2)
    sum_cross(0, 3)

    def finish_forward(chunk):
        rows = rows_of(chunk)
        total = sum_total(0, chunk)
        shift_v[0, chunk] = (act_v[rows, :].astype(F32) + total).astype(BF16)
        send(("shift", 0, chunk), shift_v.at[0, chunk], next_out.at[rows], to_next)

    def norm_grad(values, total):
        factor = lax.rsqrt(jnp.mean(values * values, axis=-1, keepdims=True) + EPSILON)
        grads = total * gain_v[...]
        inner = jnp.sum(grads * values, axis=-1, keepdims=True) * (factor * factor * factor)
        return grads * factor - values * (inner * (1.0 / WIDTH))

    def finish_far(chunk):
        rows = rows_of(chunk)
        grad = norm_grad(far_back_v[rows, :].astype(F32), plane_sum(1, chunk, 1))
        zsend[1, chunk] = grad.astype(BF16)
        send(("shift far", chunk), zsend.at[1, chunk], prev_far_out.at[rows], to_prev_far)

    def finish_own(chunk):
        rows = rows_of(chunk)
        grad = norm_grad(back_v[rows, :].astype(F32), plane_sum(1, chunk, 0))
        upstream = gath[UP, plane, y, rows].astype(F32)
        shift_v[1, chunk] = (upstream + grad).astype(BF16)
        send(("shift", 1, chunk), shift_v.at[1, chunk], prev_out.at[rows], to_prev)

    for tag in (1, 0):
        for chunk in range(CHUNKS):
            sum_near(1, chunk, tag)
    for chunk in range(CHUNKS):
        finish_forward(chunk)
    for chunk in range(CHUNKS):
        finish_far(chunk)
    for chunk in range(CHUNKS):
        finish_own(chunk)

    kept_copy.wait()
    held_copy.wait()
    for copy in sends:
        copy.wait_send()
    for chunk in range(CHUNKS):
        receive(("shift", 0, chunk), next_out.at[rows_of(chunk)])
        receive(("shift", 1, chunk), prev_out.at[rows_of(chunk)])
        receive(("shift far", chunk), prev_far_out.at[rows_of(chunk)])


def relay(act, up, stash, guest, gain, query, keyval, output, marks):
    block = jax.ShapeDtypeStruct((ROWS, WIDTH), BF16)
    anywhere = pl.BlockSpec(memory_space=pl.ANY)
    count = len(COPIES)
    vmem = pltpu.VMEM
    return pl.pallas_call(
        relay_kernel,
        out_shape=(block,) * 5,
        in_specs=[anywhere] * 9,
        out_specs=(anywhere,) * 5,
        scratch_shapes=[
            vmem((3, 2, 4, ROWS, WIDTH), BF16),
            vmem((2, 2, 4, CHUNKS, CHUNK, WIDTH), BF16),
            vmem((2, CHUNKS, 2, 2, CHUNK, HALF), BF16),
            vmem((2, CHUNKS, 2, 2, CHUNK, WIDTH), BF16),
            vmem((2, CHUNKS, CHUNK, WIDTH), BF16),
            vmem((2, CHUNKS, CHUNK, WIDTH), BF16),
            vmem((ROWS, WIDTH), BF16),
            vmem((ROWS, WIDTH), BF16),
            vmem((ROWS, WIDTH), BF16),
            vmem((ROWS, WIDTH), BF16),
            vmem((ROWS, WIDTH), BF16),
            vmem((1, WIDTH), F32),
            vmem((BLOCKS, 32), jnp.int32),
            vmem((2 * WIDTH, HEAD_DIM), BF16),
            vmem((WIDTH, CCOLS), BF16),
            vmem((QCOLS, WIDTH), BF16),
            vmem((2, LENGTH, CCOLS), BF16),
            vmem((LENGTH, QCOLS), BF16),
            vmem((LENGTH, QCOLS), BF16),
            vmem((LENGTH, CCOLS), BF16),
            vmem((2, PACKED, WIDTH), BF16),
            vmem((2, PACKED, WIDTH), BF16),
            vmem((ROWS, WIDTH), BF16),
            vmem((ROWS, WIDTH), BF16),
            vmem((2, CHUNKS, CHUNK, WIDTH), BF16),
            pltpu.SemaphoreType.DMA((count,)),
            pltpu.SemaphoreType.DMA((count,)),
            pltpu.SemaphoreType.DMA((11,)),
        ],
        compiler_params=pltpu.CompilerParams(
            collective_id=0, has_side_effects=True, vmem_limit_bytes=60 * 2**20
        ),
    )(act, up, stash, guest, gain, query, keyval, output, marks)


def finish_kernel(
    next_in,
    prev_in,
    prev_far_in,
    held_in,
    kept_in,
    next_out,
    prev_out,
    kept_out,
    held_out,
    next_v,
    prev_v,
    prev_far_v,
    held_v,
    kept_v,
    sem,
):
    section = lax.axis_index("section")
    arrivals = (
        (next_in, next_v),
        (prev_in, prev_v),
        (prev_far_in, prev_far_v),
        (held_in, held_v),
        (kept_in, kept_v),
    )
    loads = []
    for number, (source, target) in enumerate(arrivals):
        loads.append(pltpu.make_async_copy(source, target, sem.at[number]))
        loads[-1].start()
    stores = []

    def store(source, target):
        stores.append(pltpu.make_async_copy(source, target, sem.at[5 + len(stores)]))
        stores[-1].start()

    loads[0].wait()
    next_v[...] = jnp.where(section == 0, 0.0, next_v[...].astype(F32)).astype(BF16)
    store(next_v, next_out)
    loads[1].wait()
    loads[2].wait()
    total = prev_v[...].astype(F32) + prev_far_v[...].astype(F32)
    prev_v[...] = jnp.where(section == 31, 0.0, total).astype(BF16)
    store(prev_v, prev_out)
    loads[3].wait()
    store(held_v, held_out)
    loads[4].wait()
    store(kept_v, kept_out)
    for copy in stores:
        copy.wait()


def finish(*raw):
    block = jax.ShapeDtypeStruct((ROWS, WIDTH), BF16)
    anywhere = pl.BlockSpec(memory_space=pl.ANY)
    return pl.pallas_call(
        finish_kernel,
        out_shape=(block,) * 4,
        in_specs=[anywhere] * 5,
        out_specs=(anywhere,) * 4,
        scratch_shapes=[pltpu.VMEM((ROWS, WIDTH), BF16)] * 5 + [pltpu.SemaphoreType.DMA((9,))],
        compiler_params=pltpu.CompilerParams(vmem_limit_bytes=60 * 2**20),
    )(*raw)


def local(
    activations,
    upstream_grad,
    stash_blocks,
    guest_blocks,
    norm_gain,
    query_weight,
    keyval_weight,
    output_weight,
    evict_marks,
):
    raw = relay(
        activations[0],
        upstream_grad[0],
        stash_blocks[0],
        guest_blocks[0],
        norm_gain,
        query_weight[0],
        keyval_weight[0].reshape(2 * WIDTH, HEAD_DIM),
        output_weight[0],
        evict_marks.T,
    )
    return tuple(rows[None] for rows in finish(*raw))


def solution(mesh):
    placed = (
        P("section", "tensor", None),
        P("section", "tensor", None),
        P("section", "tensor", None),
        P("section", "tensor", None),
        P("section", None),
        P("section", None, "tensor"),
        P("section", None, None, "tensor"),
        P("section", "tensor", None),
        P(),
    )
    return jax.shard_map(
        local,
        mesh=mesh,
        in_specs=placed,
        out_specs=(P("section", "tensor", None),) * 4,
        check_vma=False,
    )
```
